32 devices in a mesh: tp: 2 (over y), req: 16 (over z, x, core).
Axes of the slice: x: 2, y: 2, z: 4, core: 2. Of those that a mesh axis runs over, the one named last changes fastest.
Arguments:
- token_ids: int32 [8192], P('req'), may hold values from 0 to 31999, as said below
- prompt_lengths: int32 [16, 4], P('req'), may hold values from 1 to 256, 512 in all within a row
- tenant_ids: int32 [16, 4], P('req'), may hold values from 0 to 1, never falling along the last dimension, each value on 1 to 3 neighbouring positions
- embed_table: bfloat16 [32000, 1536], P('req'), may hold values from -6 to 6
- attention_gain: float32 [1536], replicated, may hold values from 0.1 to 1.9
- qkv_weight: float32 [1536, 3072], P(('tp', 'req')), may hold values from -0.25 to 0.25
- out_weight: bfloat16 [1536, 1536], P('tp'), may hold values from -0.15625 to 0.15625
- ffn_gain: float32 [1536], replicated, may hold values from 0.1 to 1.9
- gate_up_weight: float32 [1536, 8192], P(('tp', 'req')), may hold values from -0.15625 to 0.15625
- down_weight: bfloat16 [4096, 1536], P('tp'), may hold values from -0.09375 to 0.09375
Outputs:
- final_hidden: bfloat16 [8192, 1536], P('req')
- kv_cache: bfloat16 [2, 8192, 768], P(None, 'req', 'tp')
The draws below stay inside these ranges and needn't reach their ends.
Inputs may be any that keep to these rules, and one draw needn't show every extreme that they name: Split token_ids into aligned blocks of 256 tokens and the ids into ranges of 2000 consecutive ids: no block has more than 32 ids in one range, and one range gets exactly 32 ids from every block. `prompt_lengths`: the 4 lengths of a request group sum to 512. `tenant_ids`: never falling along the prompts of a request group; every tenant has one to 3 prompts.
All inputs are finite; a program needn't handle non-finite values.
Results may differ from the reference program's by a relative error of at most 0.01.
Values may be sent and summed in bfloat16 or wider, within the bound.
No kernel may reach another device: no remote copies, remote signals or barrier semaphores. Data moves between devices by JAX's collectives and lax.ppermute only.
A program may use at most 128 MiB of HBM per device.

```python
import math
import jax
import jax.numpy as jnp
import numpy as np
from jax import lax

D = 1536
HEADS = 16
KV_HEADS = 8
HEAD_DIM = 96
FF = 4096
VOCAB = 32000
TOK_DEV = 512
PROMPTS_DEV = 4
TENANTS = 2
GROUPS = 16
TOKENS = 8192
LOOK = 256
CAP = 32
OWN_ROWS = 2000
N_TP = 2


def draw_token_ids(key, part):
    block_count = TOKENS // LOOK
    full_owner = jax.random.randint(jax.random.fold_in(key, 11), (), 0, GROUPS).astype(jnp.int32)
    other_owners = jnp.repeat(jnp.arange(GROUPS - 1, dtype=jnp.int32), CAP)

    def one_block(block_key):
        spare_owners = jax.random.permutation(jax.random.fold_in(block_key, 1), other_owners)[:LOOK - CAP]
        spare_owners = spare_owners + (spare_owners >= full_owner).astype(jnp.int32)
        owners = jnp.concatenate([jnp.full((CAP,), full_owner, jnp.int32), spare_owners])
        return jax.random.permutation(jax.random.fold_in(block_key, 2), owners)
    block_keys = jax.random.split(jax.random.fold_in(key, 12), block_count)
    owners = jax.vmap(one_block)(block_keys).reshape(TOKENS)
    row_in_range = jax.random.randint(jax.random.fold_in(key, 13), (TOKENS,), 0, OWN_ROWS).astype(jnp.int32)
    return (owners * OWN_ROWS + row_in_range).astype(jnp.int32)


def draw_embed_table(key, part):
    base = jax.random.normal(jax.random.fold_in(key, 1), (VOCAB, D), jnp.float32)
    table = base
    return jnp.clip(table, -6.0, 6.0).astype(jnp.bfloat16)


def draw_qkv_weight(key, part):
    q_full = HEADS * HEAD_DIM
    kv_full = KV_HEADS * HEAD_DIM
    base = jax.random.normal(jax.random.fold_in(key, 3), (D, q_full + 2 * kv_full), jnp.float32) / math.sqrt(D)
    return jnp.clip(base, -0.25, 0.25)


def steps_of(own_key, shape, cuts, smallest, top_value):
    factor_of = 1.0
    for position, parts in cuts:
        heights = jax.random.uniform(jax.random.fold_in(jax.random.fold_in(own_key, 6), position), (parts,), jnp.float32, smallest / len(cuts), top_value / len(cuts))
        factor_of = factor_of * jnp.repeat(jnp.exp(heights), shape[position] // parts).reshape((-1,) + (1,) * (len(shape) - 1 - position))
    return factor_of


def profile(amount, total, bound, slope):
    loads = [(1 << 20) // math.isqrt(grade ** slope) + 1 for grade in range(2, amount + 1)]
    spare, counts = total - bound - (amount - 1), [1] * (amount - 1)
    while spare > 0:
        movable = [i for i in range(amount - 1) if counts[i] < bound]
        mass, left = sum([loads[i] for i in movable]), spare
        for i in movable:
            extra = min(bound - counts[i], max(1, left * loads[i] // mass), spare)
            counts[i] = counts[i] + extra
            spare = spare - extra
    return np.array([bound] + counts)


def uneven_parts(rng, number_of, total, reach, skew):
    if number_of == 2:
        one = jax.random.randint(rng, (), max(1, total - reach), min(reach, total - 1) + 1)
        return jnp.stack([one, total - one])
    sizes = jnp.asarray(profile(number_of, total, reach, skew), jnp.int32)
    pairs = (number_of - 1) // 2
    giver, sink = sizes[1:1 + 2 * pairs:2], sizes[2:2 + 2 * pairs:2]
    room = jnp.minimum(giver - 1, reach - sink)
    moved = jax.random.randint(jax.random.fold_in(rng, 1), (pairs,), 0, 1 << 20) % (room + 1)
    sizes = sizes.at[1:1 + 2 * pairs:2].set(giver - moved).at[2:2 + 2 * pairs:2].set(sink + moved)
    return sizes[jax.random.permutation(jax.random.fold_in(rng, 2), number_of)]


def normal_values(rng, shape, scale, most, shards=(), held_as=jnp.bfloat16):
    values = scale * jax.random.normal(rng, shape, jnp.float32)
    if shards:
        values = values * steps_of(rng, shape, shards, -0.22, 0.18)
    return jnp.clip(values, -most, most).astype(held_as)


def setup_inputs(seed: int = 0) -> dict:
    streams_of = jax.random.split(jax.random.key(seed), 11)
    return {
        "token_ids": draw_token_ids(jax.random.fold_in(streams_of[10], 71), 0),
        "prompt_lengths": jax.vmap(lambda own: uneven_parts(own, PROMPTS_DEV, TOK_DEV, TOK_DEV // 2, 1))(jax.random.split(streams_of[1], GROUPS)).reshape((GROUPS, PROMPTS_DEV)).astype(jnp.int32),
        "tenant_ids": jax.vmap(lambda own: jnp.searchsorted(jnp.cumsum(uneven_parts(own, TENANTS, PROMPTS_DEV, PROMPTS_DEV - 1, 0)), jnp.arange(PROMPTS_DEV), side="right"))(jax.random.split(streams_of[2], GROUPS)).reshape((GROUPS, PROMPTS_DEV)).astype(jnp.int32),
        "embed_table": draw_embed_table(jax.random.fold_in(streams_of[10], 71), 0),
        "attention_gain": jnp.clip(1.0 + 0.18 * jax.random.normal(streams_of[4], (D,), jnp.float32), 0.1, 1.9),
        "qkv_weight": draw_qkv_weight(jax.random.fold_in(streams_of[10], 71), 0),
        "out_weight": normal_values(streams_of[6], (HEADS * HEAD_DIM, D), (HEADS * HEAD_DIM) ** -0.5, 0.15625, ((0, 2),)),
        "ffn_gain": jnp.clip(1.0 + 0.18 * jax.random.normal(streams_of[7], (D,), jnp.float32), 0.1, 1.9),
        "gate_up_weight": normal_values(streams_of[8], (D, 2 * FF), D ** -0.5, 0.15625, ((0, 32),), jnp.float32),
        "down_weight": normal_values(streams_of[9], (FF, D), FF ** -0.5, 0.09375, ((0, 2),)),
    }


rope_base = 100000.0
norm_eps = 1e-05

def rms_scaled(values, gain):
    mean_square = lax.optimization_barrier(jnp.mean(values * values, axis=-1, keepdims=True))
    return (values * lax.rsqrt(mean_square + norm_eps) * gain).astype(jnp.bfloat16)

def token_layout(lengths, tenants, row_count):
    positions = jnp.arange(row_count, dtype=jnp.int32)
    prompt_ends = jnp.cumsum(lengths).astype(jnp.int32)
    prompt_starts = prompt_ends - lengths
    passed = (positions[:, None] >= prompt_ends[None, :]).astype(jnp.int32)
    prompt = lax.optimization_barrier(jnp.sum(passed, axis=1))
    in_prompt = (prompt[:, None] == jnp.arange(lengths.shape[0], dtype=jnp.int32)[None, :]).astype(jnp.int32)
    offset = positions - lax.optimization_barrier(jnp.sum(in_prompt * prompt_starts[None, :], axis=1))
    tenant = lax.optimization_barrier(jnp.sum(in_prompt * tenants[None, :], axis=1))
    return (offset, tenant)

def rotate(values, offset):
    half_dim = values.shape[-1] // 2
    frequency = rope_base ** (-2.0 * jnp.arange(half_dim, dtype=jnp.float32) / values.shape[-1])
    angles = offset.astype(jnp.float32)[:, None] * frequency[None, :]
    cosine = jnp.cos(angles)[:, None, :]
    sine_part = jnp.sin(angles)[:, None, :]
    lower_half = values[..., :half_dim]
    upper_half = values[..., half_dim:]
    return jnp.concatenate([lower_half * cosine - upper_half * sine_part, upper_half * cosine + lower_half * sine_part], axis=-1)

def attend(queries, key_heads, value_heads, tenant):
    row_count = queries.shape[0]
    block_rows = min(512, row_count)
    positions = jnp.arange(row_count, dtype=jnp.int32)
    score_scale = queries.shape[-1] ** (-0.5)
    pieces = []
    for start_row in range(0, row_count, block_rows):
        query_pos = positions[start_row:start_row + block_rows]
        allowed = (positions[None, :] <= query_pos[:, None]) & (tenant[None, :] == tenant[start_row:start_row + block_rows][:, None])
        scores = jnp.einsum('qkgd,skd->kgqs', queries[start_row:start_row + block_rows].astype(jnp.float32), key_heads.astype(jnp.float32)) * score_scale
        scores = jnp.where(allowed[None, None], scores, -jnp.inf)
        row_max = lax.optimization_barrier(jnp.max(scores, axis=-1, keepdims=True))
        expo = jnp.exp(scores - row_max)
        weights = (expo / lax.optimization_barrier(jnp.sum(expo, axis=-1, keepdims=True))).astype(jnp.bfloat16)
        mixed_out = jnp.einsum('kgqs,skd->qkgd', weights.astype(jnp.float32), value_heads.astype(jnp.float32))
        pieces.append(mixed_out.astype(jnp.bfloat16))
    return jnp.concatenate(pieces, axis=0)

def rounded_sum(left, right, block_width):
    total = jnp.zeros((left.shape[0], right.shape[1]), jnp.float32)
    for block in range(N_TP):
        term = jnp.dot(left[:, block * block_width:(block + 1) * block_width], right[block * block_width:(block + 1) * block_width], preferred_element_type=jnp.float32)
        term = lax.optimization_barrier(term.astype(jnp.bfloat16))
        total = total + term.astype(jnp.float32)
    return total

def reference(token_ids, prompt_lengths, tenant_ids, embed_table, attention_gain, qkv_weight, out_weight, ffn_gain, gate_up_weight, down_weight):
    embedded_all = jnp.take(embed_table, token_ids, axis=0).reshape(GROUPS, TOK_DEV, D)
    packed = qkv_weight.astype(jnp.bfloat16)
    gate_up_bf = gate_up_weight.astype(jnp.bfloat16)
    q_full = HEADS * HEAD_DIM
    kv_full = KV_HEADS * HEAD_DIM

    def one_group(items):
        embedded, lengths, tenants = items
        offset, tenant = token_layout(lengths, tenants, TOK_DEV)
        normed = rms_scaled(embedded.astype(jnp.float32), attention_gain)
        projected = jnp.dot(normed, packed, preferred_element_type=jnp.float32)
        queries = rotate(projected[:, :q_full].reshape(TOK_DEV, HEADS, HEAD_DIM), offset).astype(jnp.bfloat16)
        key_heads = rotate(projected[:, q_full:q_full + kv_full].reshape(TOK_DEV, KV_HEADS, HEAD_DIM), offset).astype(jnp.bfloat16)
        value_heads = projected[:, q_full + kv_full:].reshape(TOK_DEV, KV_HEADS, HEAD_DIM).astype(jnp.bfloat16)
        attended = attend(queries.reshape(TOK_DEV, KV_HEADS, HEADS // KV_HEADS, HEAD_DIM), key_heads, value_heads, tenant).reshape(TOK_DEV, q_full)
        residual = embedded.astype(jnp.float32) + rounded_sum(attended, out_weight, q_full // N_TP)
        normed_ffn = rms_scaled(residual, ffn_gain)
        gate_up = jnp.dot(normed_ffn, gate_up_bf, preferred_element_type=jnp.float32)
        hidden = (jax.nn.silu(gate_up[:, :FF]) * gate_up[:, FF:]).astype(jnp.bfloat16)
        final_out = (residual + rounded_sum(hidden, down_weight, FF // N_TP)).astype(jnp.bfloat16)
        kv_cache = jnp.stack([key_heads.reshape(TOK_DEV, kv_full), value_heads.reshape(TOK_DEV, kv_full)])
        return (final_out, kv_cache)
    final_all, cache_all = lax.map(one_group, (embedded_all, prompt_lengths, tenant_ids))
    return (final_all.reshape(TOKENS, D), cache_all.transpose(1, 0, 2, 3).reshape(2, TOKENS, kv_full))
```

```python
import jax
import jax.numpy as jnp
from jax import lax
from jax.sharding import PartitionSpec as P

HEAD_DIM = 96


rope_base = 100000.0
norm_eps = 1e-05


def rms_scaled(values, gain):
    mean_square = jnp.mean(values * values, axis=-1, keepdims=True)
    return (values * lax.rsqrt(mean_square + norm_eps) * gain).astype(jnp.bfloat16)


def token_layout(lengths, tenants, row_count):
    positions = jnp.arange(row_count, dtype=jnp.int32)
    prompt_ends = jnp.cumsum(lengths)
    prompt_starts = prompt_ends - lengths
    passed = (positions[:, None] >= prompt_ends[None, :]).astype(jnp.int32)
    prompt = jnp.sum(passed, axis=1)
    in_prompt = (prompt[:, None] == jnp.arange(lengths.shape[0], dtype=jnp.int32)[None, :]).astype(
        jnp.int32
    )
    offset = positions - jnp.sum(in_prompt * prompt_starts[None, :], axis=1)
    tenant = jnp.sum(in_prompt * tenants[None, :], axis=1)
    return (offset, tenant)


def rotate(values, offset):
    half_dim = values.shape[-1] // 2
    frequency = rope_base ** (-2.0 * jnp.arange(half_dim, dtype=jnp.float32) / values.shape[-1])
    angles = offset.astype(jnp.float32)[:, None] * frequency[None, :]
    cosine = jnp.cos(angles)[:, None, :]
    sine_part = jnp.sin(angles)[:, None, :]
    lower_half = values[..., :half_dim]
    upper_half = values[..., half_dim:]
    return jnp.concatenate(
        [
            lower_half * cosine - upper_half * sine_part,
            upper_half * cosine + lower_half * sine_part,
        ],
        axis=-1,
    )


def attend(queries, key_heads, value_heads, tenant):
    row_count = queries.shape[0]
    positions = jnp.arange(row_count, dtype=jnp.int32)
    score_scale = queries.shape[-1] ** (-0.5)
    allowed = (positions[None, :] <= positions[:, None]) & (tenant[None, :] == tenant[:, None])
    scores = (
        jnp.einsum("qkgd,skd->kgqs", queries, key_heads, preferred_element_type=jnp.float32)
        * score_scale
    )
    scores = jnp.where(allowed[None, None], scores, -jnp.inf)
    row_max = jnp.max(scores, axis=-1, keepdims=True)
    expo = jnp.exp(scores - row_max)
    weights = (expo / jnp.sum(expo, axis=-1, keepdims=True)).astype(jnp.bfloat16)
    mixed_out = jnp.einsum(
        "kgqs,skd->qkgd", weights, value_heads, preferred_element_type=jnp.float32
    )
    pieces = mixed_out.astype(jnp.bfloat16)
    return pieces


PAIR = [(0, 1), (1, 0)]


def two_part_dot(left, right, split, tp_index):
    width = right.shape[1] // 2
    own = lax.dynamic_slice_in_dim(left, tp_index * split, split, axis=1)
    other = lax.dynamic_slice_in_dim(left, (1 - tp_index) * split, split, axis=1)
    return jnp.dot(own, right[:, :width], preferred_element_type=jnp.float32) + jnp.dot(
        other, right[:, width:], preferred_element_type=jnp.float32
    )


def in_order(own, other, tp_index, axis):
    first = jnp.where(tp_index == 0, own, other)
    second = jnp.where(tp_index == 0, other, own)
    return jnp.concatenate([first, second], axis=axis)


def per_device(
    token_ids,
    prompt_lengths,
    tenant_ids,
    embed_table,
    attention_gain,
    qkv_weight,
    out_weight,
    ffn_gain,
    gate_up_weight,
    down_weight,
):
    tp_count = lax.axis_size("tp")
    tp_index = lax.axis_index("tp")
    group_count = lax.axis_size("req")
    tokens = token_ids.shape[0]
    looked = tokens // tp_count
    own_rows = embed_table.shape[0]
    width = embed_table.shape[1]
    capacity = max(2, 2 * looked // group_count)
    q_half = out_weight.shape[0]
    ff_half = down_weight.shape[0]
    q_full = q_half * tp_count
    kv_half = (qkv_weight.shape[1] - q_full) // (2 * tp_count)
    kv_full = kv_half * tp_count
    ff_full = ff_half * tp_count
    half_width = width // tp_count

    def qkv_cols(half):
        return jnp.concatenate(
            [
                lax.dynamic_slice_in_dim(qkv_weight, base + half * size, size, axis=1)
                for base, size in ((0, q_half), (q_full, kv_half), (q_full + kv_full, kv_half))
            ],
            axis=1,
        ).astype(jnp.bfloat16)

    def ffn_cols(half):
        return jnp.concatenate(
            [
                lax.dynamic_slice_in_dim(gate_up_weight, base + half * ff_half, ff_half, axis=1)
                for base in (0, ff_full)
            ],
            axis=1,
        ).astype(jnp.bfloat16)

    other_qkv = lax.ppermute(qkv_cols(1 - tp_index), "tp", PAIR)
    qkv_all = lax.all_gather(
        jnp.concatenate([qkv_cols(tp_index), other_qkv], axis=1), "req", axis=0, tiled=True
    )
    other_ffn = lax.ppermute(ffn_cols(1 - tp_index), "tp", PAIR)
    ffn_all = lax.all_gather(
        jnp.concatenate([ffn_cols(tp_index), other_ffn], axis=1), "req", axis=0, tiled=True
    )
    out_other = lax.ppermute(out_weight, "tp", PAIR)

    my_ids = lax.dynamic_slice_in_dim(token_ids, tp_index * looked, looked)
    owner_of = my_ids // own_rows
    row_in_range = my_ids - owner_of * own_rows
    owners = jnp.arange(group_count, dtype=jnp.int32)
    owner_hits = owner_of[:, None] == owners[None, :]
    earlier = jnp.arange(looked)[None, :] < jnp.arange(looked)[:, None]
    same = (owner_of[:, None] == owner_of[None, :]) & earlier
    slot_of = jnp.sum(same.astype(jnp.int32), axis=1)
    place = owner_of * capacity + slot_of
    chosen = place[None, :] == jnp.arange(group_count * capacity, dtype=jnp.int32)[:, None]
    requests = (
        jnp.sum(jnp.where(chosen, row_in_range[None, :] + 1, 0), axis=1).reshape(
            group_count, capacity
        )
        - 1
    )
    asked = lax.all_to_all(requests, "req", split_axis=0, concat_axis=0, tiled=True).reshape(-1)
    pick_rows = (asked[:, None] == jnp.arange(own_rows, dtype=jnp.int32)[None, :]).astype(
        jnp.bfloat16
    )
    found_rows = jnp.dot(pick_rows, embed_table, preferred_element_type=jnp.float32).astype(
        jnp.bfloat16
    )
    returned = lax.all_to_all(
        found_rows.reshape(group_count, capacity, width),
        "req",
        split_axis=0,
        concat_axis=0,
        tiled=True,
    ).reshape(group_count * capacity, width)
    pick_mine = (
        place[:, None] == jnp.arange(group_count * capacity, dtype=jnp.int32)[None, :]
    ).astype(jnp.bfloat16)
    embedded_own = jnp.dot(pick_mine, returned, preferred_element_type=jnp.float32).astype(
        jnp.bfloat16
    )
    embedded_other = lax.ppermute(embedded_own, "tp", PAIR)
    embedded = in_order(embedded_own, embedded_other, tp_index, 0).astype(jnp.float32)

    offset, tenant = token_layout(prompt_lengths[0], tenant_ids[0], tokens)
    normed = rms_scaled(embedded, attention_gain)
    projected = two_part_dot(normed, qkv_all, half_width, tp_index)
    kv_local = kv_half // HEAD_DIM
    queries = rotate(
        projected[:, :q_half].reshape(tokens, q_half // HEAD_DIM, HEAD_DIM), offset
    ).astype(jnp.bfloat16)
    key_heads = rotate(
        projected[:, q_half : q_half + kv_half].reshape(tokens, kv_local, HEAD_DIM), offset
    ).astype(jnp.bfloat16)
    value_heads = (
        projected[:, q_half + kv_half :].reshape(tokens, kv_local, HEAD_DIM).astype(jnp.bfloat16)
    )
    kv_cache = jnp.stack([key_heads.reshape(tokens, kv_half), value_heads.reshape(tokens, kv_half)])
    attended = attend(
        queries.reshape(tokens, kv_local, -1, HEAD_DIM), key_heads, value_heads, tenant
    ).reshape(tokens, q_half)
    attended_other = lax.ppermute(attended, "tp", PAIR)
    residual = (
        embedded
        + jnp.dot(attended, out_weight, preferred_element_type=jnp.float32)
        + jnp.dot(attended_other, out_other, preferred_element_type=jnp.float32)
    )
    normed_ffn = rms_scaled(residual, ffn_gain)
    gate_up = two_part_dot(normed_ffn, ffn_all, half_width, tp_index)
    hidden = (jax.nn.silu(gate_up[:, :ff_half]) * gate_up[:, ff_half:]).astype(jnp.bfloat16)
    chunks = 4
    step = width // chunks
    finals = []
    for c in range(chunks):
        part = jnp.dot(
            hidden, down_weight[:, c * step : (c + 1) * step], preferred_element_type=jnp.float32
        ).astype(jnp.bfloat16)
        total = part.astype(jnp.float32) + lax.ppermute(part, "tp", PAIR).astype(jnp.float32)
        finals.append((residual[:, c * step : (c + 1) * step] + total).astype(jnp.bfloat16))
    return (jnp.concatenate(finals, axis=1), kv_cache)


def solution(mesh):
    return jax.shard_map(
        per_device,
        mesh=mesh,
        in_specs=(
            P("req"),
            P("req", None),
            P("req", None),
            P("req", None),
            P(),
            P(("tp", "req"), None),
            P("tp", None),
            P(),
            P(("tp", "req"), None),
            P("tp", None),
        ),
        out_specs=(P("req", None), P(None, "req", "tp")),
        check_vma=False,
    )
```

```python
import functools
import math

import jax
import jax.numpy as jnp
from jax import lax
from jax.experimental import pallas as pl
from jax.experimental.pallas import tpu as pltpu
from jax.sharding import PartitionSpec as P

HEAD_DIM = 96
HALF = HEAD_DIM // 2
LANES = 128

rope_base = 100000.0
norm_eps = 1e-05

BF = jnp.bfloat16
F32 = jnp.float32
PAIR = [(0, 1), (1, 0)]
VMEM_LIMIT = 48 * 1024 * 1024


def token_layout(lengths, tenants, row_count):
    positions = jnp.arange(row_count, dtype=jnp.int32)
    ends, offset, tenant, start = 0, positions, jnp.full_like(positions, 0), 0
    for i in range(lengths.shape[0]):
        inside = positions >= start
        offset = jnp.where(inside, positions - start, offset)
        tenant = jnp.where(inside, tenants[i], tenant)
        start = start + lengths[i]
    return (offset, tenant)


def chip_ring(chips):
    order = list(range(0, chips, 2)) + list(range(chips - 1 - chips % 2, 0, -2))
    following = {order[i]: order[(i + 1) % chips] for i in range(chips)}
    pairs = [(2 * c, 2 * d) for c, d in following.items()]
    pairs += [(2 * d + 1, 2 * c + 1) for c, d in following.items()]
    return order, pairs


def ring_gather(block, pairs, chips):
    blocks = [block]
    for _ in range(chips - 1):
        blocks.append(lax.ppermute(blocks[-1], "req", pairs))
    return blocks


def whole(shape):
    return pl.BlockSpec(shape, lambda: (0,) * len(shape), memory_space=pltpu.VMEM)


def in_vmem(count):
    return [pl.BlockSpec(memory_space=pltpu.VMEM)] * count


def params():
    return pltpu.CompilerParams(vmem_limit_bytes=VMEM_LIMIT)


def spread_columns(heads):
    column = jnp.arange(heads * HEAD_DIM, dtype=jnp.int32)
    within = column % HEAD_DIM
    target = column // HEAD_DIM * LANES + jnp.where(within < HALF, within, within + 64 - HALF)
    return (target[:, None] == jnp.arange(heads * LANES, dtype=jnp.int32)[None, :]).astype(BF)


def prep_kernel(chips, place_ref, *refs):
    blocks = refs[: chips + 1]
    spread_ref, out_ref, raw, sems = refs[chips + 1 :]
    copies = []
    for s in range(chips):
        copies.append(pltpu.make_async_copy(blocks[s], raw.at[place_ref[s]], sems.at[s]))
    for s in range(chips):
        copies.append(
            pltpu.make_async_copy(
                blocks[chips].at[s], raw.at[place_ref[chips + s]], sems.at[chips + s]
            )
        )
    for copy in copies:
        copy.start()
    for copy in copies:
        copy.wait()
    count, rows, _ = raw.shape
    narrow, wide = spread_ref.shape
    for b in range(raw.shape[2] // narrow):
        part = raw[:, :, b * narrow : (b + 1) * narrow].reshape(count * rows, narrow)
        out_ref[:, b * wide : (b + 1) * wide] = jnp.dot(
            part, spread_ref[...], preferred_element_type=F32
        ).astype(BF)


def prepare_qkv(place, blocks, got, spread):
    chips = len(blocks)
    rows, cols = blocks[0].shape
    wide = cols // spread.shape[0] * spread.shape[1]
    return pl.pallas_call(
        functools.partial(prep_kernel, chips),
        out_shape=jax.ShapeDtypeStruct((2 * chips * rows, wide), BF),
        in_specs=[pl.BlockSpec(memory_space=pltpu.SMEM)]
        + [pl.BlockSpec(memory_space=pl.ANY)] * (chips + 1)
        + in_vmem(1),
        out_specs=pl.BlockSpec(memory_space=pltpu.VMEM),
        scratch_shapes=[
            pltpu.VMEM((2 * chips, rows, cols), BF),
            pltpu.SemaphoreType.DMA((2 * chips,)),
        ],
        compiler_params=params(),
        name="prepare_qkv",
        cost_estimate=pl.CostEstimate(
            flops=4 * chips * rows * cols * spread.shape[1],
            bytes_accessed=8 * chips * rows * cols,
            transcendentals=0,
        ),
    )(place, *blocks, got, spread)


def attention_kernel(
    q_heads,
    kv_heads,
    emb_ref,
    gain_ref,
    weight_ref,
    cos_ref,
    sin_ref,
    ten_col_ref,
    ten_row_ref,
    pack_ref,
    att_ref,
    cache_ref,
    normed,
    keys,
    values,
    mixed,
    bias,
):
    tokens = emb_ref.shape[0]
    step = tokens // 2
    group = q_heads // kv_heads
    for r in range(0, tokens, step):
        x = emb_ref[r : r + step, :].astype(F32)
        scale = lax.rsqrt(jnp.mean(x * x, axis=-1, keepdims=True) + norm_eps)
        normed[r : r + step, :] = (x * scale * gain_ref[...]).astype(BF)
        row = lax.broadcasted_iota(jnp.int32, (step, tokens), 0) + r
        col = lax.broadcasted_iota(jnp.int32, (step, tokens), 1)
        allowed = (col <= row) & (ten_col_ref[r : r + step, :] == ten_row_ref[...])
        bias[r : r + step, :] = jnp.where(allowed, 0.0, -1e30)

    def turned(x):
        return (x * cos_ref[...] + pltpu.roll(x, 64, 1) * sin_ref[...]).astype(BF)

    def project(first, heads):
        return jnp.dot(
            normed[...],
            weight_ref[:, first * LANES : (first + heads) * LANES],
            preferred_element_type=F32,
        )

    k_all = project(q_heads, kv_heads)
    for h in range(kv_heads):
        keys[:, h * LANES : (h + 1) * LANES] = turned(k_all[:, h * LANES : (h + 1) * LANES])
    values[...] = project(q_heads + kv_heads, kv_heads).astype(BF)
    factor = HEAD_DIM**-0.5 * math.log2(math.e)
    for kv in range(kv_heads):
        lanes = slice(kv * LANES, (kv + 1) * LANES)
        q_all = project(kv * group, group)
        for g in range(group):
            q = turned(q_all[:, g * LANES : (g + 1) * LANES])
            for r in range(0, tokens, step):
                seen = r + step
                scores = (
                    lax.dot_general(
                        q[r : r + step, :],
                        keys[:seen, lanes],
                        (((1,), (1,)), ((), ())),
                        preferred_element_type=F32,
                    )
                    + bias[r : r + step, :seen]
                )
                top = jnp.max(scores, axis=-1, keepdims=True)
                expo = jnp.exp2((scores - top) * factor)
                total = jnp.sum(expo, axis=-1, keepdims=True)
                out = jnp.dot(expo.astype(BF), values[:seen, lanes], preferred_element_type=F32)
                h = kv * group + g
                mixed[r : r + step, h * LANES : (h + 1) * LANES] = (out / total).astype(BF)
    wide, narrow = pack_ref.shape
    for b in range(q_heads * LANES // wide):
        att_ref[:, b * narrow : (b + 1) * narrow] = jnp.dot(
            mixed[:, b * wide : (b + 1) * wide], pack_ref[...], preferred_element_type=F32
        ).astype(BF)
    cache_ref[0] = jnp.dot(keys[...], pack_ref[...], preferred_element_type=F32).astype(BF)
    cache_ref[1] = jnp.dot(values[...], pack_ref[...], preferred_element_type=F32).astype(BF)


def attention(embedded, gain, weight, cosine, sine, tenant, pack, q_heads, kv_heads):
    tokens, width = embedded.shape
    return pl.pallas_call(
        functools.partial(attention_kernel, q_heads, kv_heads),
        out_shape=(
            jax.ShapeDtypeStruct((tokens, q_heads * HEAD_DIM), BF),
            jax.ShapeDtypeStruct((2, tokens, kv_heads * HEAD_DIM), BF),
        ),
        in_specs=in_vmem(8),
        out_specs=tuple(in_vmem(2)),
        scratch_shapes=[
            pltpu.VMEM((tokens, width), BF),
            pltpu.VMEM((tokens, kv_heads * LANES), BF),
            pltpu.VMEM((tokens, kv_heads * LANES), BF),
            pltpu.VMEM((tokens, q_heads * LANES), BF),
            pltpu.VMEM((tokens, tokens), F32),
        ],
        compiler_params=params(),
        name="attention",
        cost_estimate=pl.CostEstimate(
            flops=2 * tokens * width * weight.shape[1],
            bytes_accessed=2 * weight.size + 6 * embedded.size,
            transcendentals=q_heads * tokens * tokens,
        ),
    )(embedded, gain, weight, cosine, sine, tenant[:, None], tenant[None, :], pack)


def output_kernel(emb_ref, own_ref, other_ref, w_own_ref, w_other_ref, gain_ref, res_ref, norm_ref):
    tokens = emb_ref.shape[0]
    step = tokens // 4
    for r in range(0, tokens, step):
        rows = slice(r, r + step)
        x = (
            emb_ref[rows, :].astype(F32)
            + jnp.dot(own_ref[rows, :], w_own_ref[...], preferred_element_type=F32)
            + jnp.dot(other_ref[rows, :], w_other_ref[...], preferred_element_type=F32)
        )
        res_ref[rows, :] = x
        scale = lax.rsqrt(jnp.mean(x * x, axis=-1, keepdims=True) + norm_eps)
        norm_ref[rows, :] = (x * scale * gain_ref[...]).astype(BF)


def output_part(embedded, own, other, w_own, w_other, gain):
    tokens, width = embedded.shape
    return pl.pallas_call(
        output_kernel,
        out_shape=(
            jax.ShapeDtypeStruct((tokens, width), F32),
            jax.ShapeDtypeStruct((tokens, width), BF),
        ),
        in_specs=in_vmem(6),
        out_specs=tuple(in_vmem(2)),
        compiler_params=params(),
        name="output_part",
        cost_estimate=pl.CostEstimate(
            flops=8 * tokens * w_own.size // 2,
            bytes_accessed=4 * w_own.size + 8 * embedded.size,
            transcendentals=0,
        ),
    )(embedded, own, other, w_own, w_other, gain)


def hidden_kernel(chips, place_ref, x_ref, *refs):
    blocks = refs[: chips + 1]
    out_ref, buf, sems = refs[chips + 1 :]
    ff_half = out_ref.shape[1]
    _, _, count, rows, wide = buf.shape
    width = count * rows

    def copies(j):
        made = []
        for part in range(2):
            cols = pl.ds(part * ff_half + j * wide, wide)
            for s in range(2 * chips):
                source = (
                    blocks[s].at[:, cols] if s < chips else blocks[chips].at[s - chips, :, cols]
                )
                made.append(
                    pltpu.make_async_copy(
                        source, buf.at[j % 2, part, place_ref[s]], sems.at[j % 2, part, s]
                    )
                )
        return made

    steps = ff_half // wide
    pending = copies(0)
    for copy in pending:
        copy.start()
    for j in range(steps):
        current = pending
        if j + 1 < steps:
            pending = copies(j + 1)
            for copy in pending:
                copy.start()
        for copy in current:
            copy.wait()
        gate = jnp.dot(
            x_ref[...], buf[j % 2, 0].reshape(width, wide), preferred_element_type=F32
        )
        up = jnp.dot(x_ref[...], buf[j % 2, 1].reshape(width, wide), preferred_element_type=F32)
        out_ref[:, j * wide : (j + 1) * wide] = (gate / (1.0 + jnp.exp(-gate)) * up).astype(BF)


def hidden_part(place, normed, blocks, got):
    chips = len(blocks)
    rows, cols = blocks[0].shape
    tokens, width = normed.shape
    wide = min(512, cols // 2)
    return pl.pallas_call(
        functools.partial(hidden_kernel, chips),
        out_shape=jax.ShapeDtypeStruct((tokens, cols // 2), BF),
        in_specs=[pl.BlockSpec(memory_space=pltpu.SMEM)]
        + in_vmem(1)
        + [pl.BlockSpec(memory_space=pl.ANY)] * (chips + 1),
        out_specs=pl.BlockSpec(memory_space=pltpu.VMEM),
        scratch_shapes=[
            pltpu.VMEM((2, 2, 2 * chips, rows, wide), BF),
            pltpu.SemaphoreType.DMA((2, 2, 2 * chips)),
        ],
        compiler_params=params(),
        name="hidden_part",
        cost_estimate=pl.CostEstimate(
            flops=2 * tokens * width * cols,
            bytes_accessed=2 * width * cols + 4 * normed.size,
            transcendentals=tokens * cols // 2,
        ),
    )(place, normed, *blocks, got)


def per_device(
    token_ids,
    prompt_lengths,
    tenant_ids,
    embed_table,
    attention_gain,
    qkv_weight,
    out_weight,
    ffn_gain,
    gate_up_weight,
    down_weight,
):
    tp_count = lax.axis_size("tp")
    tp_index = lax.axis_index("tp")
    group_count = lax.axis_size("req")
    req_index = lax.axis_index("req")
    tokens = token_ids.shape[0]
    looked = tokens // tp_count
    own_rows, width = embed_table.shape
    capacity = max(2, 2 * looked // group_count)
    q_half = out_weight.shape[0]
    ff_half = down_weight.shape[0]
    q_full = q_half * tp_count
    kv_half = (qkv_weight.shape[1] - q_full) // (2 * tp_count)
    kv_full = kv_half * tp_count
    ff_full = ff_half * tp_count
    chips = group_count // 2
    core = req_index % 2
    chip = req_index // 2
    core_swap = [(i, i ^ 1) for i in range(group_count)]
    order, ring_pairs = chip_ring(chips)

    my_ids = lax.dynamic_slice_in_dim(token_ids, tp_index * looked, looked)
    owner_of = my_ids // own_rows
    row_in_range = my_ids - owner_of * own_rows
    earlier = jnp.arange(looked)[None, :] < jnp.arange(looked)[:, None]
    same = (owner_of[:, None] == owner_of[None, :]) & earlier
    place = owner_of * capacity + jnp.sum(same.astype(jnp.int32), axis=1)
    slots = jnp.arange(group_count * capacity, dtype=jnp.int32)
    chosen = place[None, :] == slots[:, None]
    requests = jnp.sum(jnp.where(chosen, row_in_range[None, :] + 1, 0), axis=1) - 1
    asked = lax.all_to_all(
        requests.reshape(group_count, capacity), "req", split_axis=0, concat_axis=0, tiled=True
    ).reshape(-1)

    def columns(weight, parts, half):
        return jnp.concatenate(
            [
                lax.dynamic_slice_in_dim(weight, base + half * size, size, axis=1)
                for base, size in parts
            ],
            axis=1,
        ).astype(BF)

    def chip_block(weight, parts):
        own = columns(weight, parts, tp_index)
        other = lax.ppermute(columns(weight, parts, 1 - tp_index), "tp", PAIR)
        kept = jnp.where(core == 0, own, other)
        moved = lax.ppermute(jnp.where(core == 0, other, own), "req", core_swap)
        return jnp.concatenate(
            [jnp.where(core == 0, kept, moved), jnp.where(core == 0, moved, kept)], axis=0
        )

    qkv_block = chip_block(
        qkv_weight, ((0, q_half), (q_full, kv_half), (q_full + kv_full, kv_half))
    )
    ffn_block = chip_block(gate_up_weight, ((0, ff_half), (ff_full, ff_half)))
    qkv_blocks = ring_gather(qkv_block, ring_pairs, chips)
    ffn_blocks = ring_gather(ffn_block, ring_pairs, chips)
    qkv_got = lax.ppermute(jnp.stack(qkv_blocks), "req", core_swap)
    ffn_got = lax.ppermute(jnp.stack(ffn_blocks), "req", core_swap)
    steps = jnp.arange(chips, dtype=jnp.int32)
    here = jnp.where(chip % 2 == 0, chip // 2, chips - 1 - chip // 2)

    def source_chip(position):
        position = position % chips
        return jnp.where(position < (chips + 1) // 2, 2 * position, 2 * (chips - 1 - position) + 1)

    up_chip, down_chip = source_chip(here - steps), source_chip(here + steps)
    mine_half = (tp_index + core) % 2
    spots = jnp.concatenate(
        [
            jnp.where(core == 0, up_chip, down_chip) + mine_half * chips,
            jnp.where(core == 0, down_chip, up_chip) + (1 - mine_half) * chips,
        ]
    )

    out_other = lax.ppermute(out_weight, "tp", PAIR)

    pick_rows = (asked[:, None] == jnp.arange(own_rows, dtype=jnp.int32)[None, :]).astype(BF)
    found_rows = jnp.dot(pick_rows, embed_table, preferred_element_type=F32).astype(BF)
    returned = lax.all_to_all(
        found_rows.reshape(group_count, capacity, width),
        "req",
        split_axis=0,
        concat_axis=0,
        tiled=True,
    ).reshape(group_count * capacity, width)
    pick_mine = (place[:, None] == slots[None, :]).astype(BF)
    embedded_own = jnp.dot(pick_mine, returned, preferred_element_type=F32).astype(BF)
    embedded_other = lax.ppermute(embedded_own, "tp", PAIR)
    embedded = jnp.concatenate(
        [
            jnp.where(tp_index == 0, embedded_own, embedded_other),
            jnp.where(tp_index == 0, embedded_other, embedded_own),
        ],
        axis=0,
    )

    offset, tenant = token_layout(prompt_lengths[0], tenant_ids[0], tokens)
    lane = jnp.arange(LANES, dtype=jnp.int32)
    index = lane % 64
    frequency = rope_base ** (-2.0 * index.astype(F32) / HEAD_DIM)
    angles = offset.astype(F32)[:, None] * frequency[None, :]
    cosine = jnp.cos(angles)
    sine = jnp.where(lane < 64, -1.0, 1.0)[None, :] * jnp.sin(angles)

    kv_local = kv_half // HEAD_DIM
    spread = spread_columns(kv_local)
    weight = prepare_qkv(spots, qkv_blocks, qkv_got, spread)
    attended, kv_cache = attention(
        embedded,
        attention_gain[None, :],
        weight,
        cosine,
        sine,
        tenant,
        spread.T,
        q_half // HEAD_DIM,
        kv_local,
    )
    attended_other = lax.ppermute(attended, "tp", PAIR)
    residual, normed_ffn = output_part(
        embedded, attended, attended_other, out_weight, out_other, ffn_gain[None, :]
    )
    hidden = hidden_part(spots, normed_ffn, ffn_blocks, ffn_got)
    chunks = 4
    step = width // chunks
    finals = []
    for c in range(chunks):
        cols = slice(c * step, (c + 1) * step)
        part = jnp.dot(hidden, down_weight[:, cols], preferred_element_type=F32).astype(BF)
        total = part.astype(F32) + lax.ppermute(part, "tp", PAIR).astype(F32)
        finals.append((residual[:, cols] + total).astype(BF))
    return (jnp.concatenate(finals, axis=1), kv_cache)


def solution(mesh):
    return jax.shard_map(
        per_device,
        mesh=mesh,
        in_specs=(
            P("req"),
            P("req", None),
            P("req", None),
            P("req", None),
            P(),
            P(("tp", "req"), None),
            P("tp", None),
            P(),
            P(("tp", "req"), None),
            P("tp", None),
        ),
        out_specs=(P("req", None), P(None, "req", "tp")),
        check_vma=False,
    )
```

```python
import functools
import math

import jax
import jax.numpy as jnp
from jax import lax
from jax.experimental import pallas as pl
from jax.experimental.pallas import tpu as pltpu
from jax.sharding import PartitionSpec as P

HEAD_DIM = 96
HALF = HEAD_DIM // 2
LANES = 128

rope_base = 100000.0
norm_eps = 1e-05

BF = jnp.bfloat16
F32 = jnp.float32
PAIR = [(0, 1), (1, 0)]
VMEM_LIMIT = 48 * 1024 * 1024


def token_offsets(starts, row_count):
    positions = jnp.arange(row_count, dtype=jnp.int32)
    offset = positions
    for i in range(1, starts.shape[0]):
        offset = jnp.where(positions >= starts[i], positions - starts[i], offset)
    return offset


def after(value, *others):
    return lax.optimization_barrier((value, *others))[0]


def chip_ring(chips):
    order = list(range(0, chips, 2)) + list(range(chips - 1 - chips % 2, 0, -2))
    following = {order[i]: order[(i + 1) % chips] for i in range(chips)}
    pairs = [(2 * c, 2 * d) for c, d in following.items()]
    pairs += [(2 * d + 1, 2 * c + 1) for c, d in following.items()]
    return order, pairs


def ring_more(blocks, count, pairs, *ready):
    blocks = list(blocks)
    for i in range(count):
        last = after(blocks[-1], *ready) if ready and i == 0 else blocks[-1]
        blocks.append(lax.ppermute(last, "req", pairs))
    return blocks


def in_vmem(count):
    return [pl.BlockSpec(memory_space=pltpu.VMEM)] * count


def params():
    return pltpu.CompilerParams(vmem_limit_bytes=VMEM_LIMIT)


def spread_columns(heads):
    column = jnp.arange(heads * HEAD_DIM, dtype=jnp.int32)
    within = column % HEAD_DIM
    target = column // HEAD_DIM * LANES + jnp.where(within < HALF, within, within + 64 - HALF)
    return (target[:, None] == jnp.arange(heads * LANES, dtype=jnp.int32)[None, :]).astype(BF)


def tenant_at(start_ref, tenant_ref, positions):
    tenant = jnp.full(positions.shape, tenant_ref[0], jnp.int32)
    for i in range(1, tenant_ref.shape[0]):
        tenant = jnp.where(positions >= start_ref[i], tenant_ref[i], tenant)
    return tenant


def bias_of(start_ref, tenant_ref, first, count, seen):
    row = lax.broadcasted_iota(jnp.int32, (count, seen), 0) + first
    col = lax.broadcasted_iota(jnp.int32, (count, seen), 1)
    query_tenant = tenant_at(
        start_ref, tenant_ref, lax.broadcasted_iota(jnp.int32, (count, 1), 0) + first
    )
    key_tenant = tenant_at(start_ref, tenant_ref, lax.broadcasted_iota(jnp.int32, (1, seen), 1))
    return jnp.where((col <= row) & (query_tenant == key_tenant), 0.0, -1e30)


def attend_head(q, keys, values, bias):
    scores = lax.dot_general(q, keys, (((1,), (1,)), ((), ())), preferred_element_type=F32) + bias
    top = jnp.max(scores, axis=-1, keepdims=True)
    expo = jnp.exp2((scores - top) * (HEAD_DIM**-0.5 * math.log2(math.e)))
    total = jnp.sum(expo, axis=-1, keepdims=True)
    out = jnp.dot(expo.astype(BF), values, preferred_element_type=F32)
    return (out / total).astype(BF)


def packed(x, pack_ref):
    wide = pack_ref.shape[0]
    return jnp.concatenate(
        [
            jnp.dot(x[:, b : b + wide], pack_ref[...], preferred_element_type=F32).astype(BF)
            for b in range(0, x.shape[1], wide)
        ],
        axis=1,
    )


def project_kernel(
    q_heads,
    kv_heads,
    blocks,
    spots_ref,
    start_ref,
    tenant_ref,
    emb_ref,
    gain_ref,
    cos_ref,
    sin_ref,
    spread_ref,
    pack_ref,
    *refs,
):
    sources, refs = block_list(refs[:blocks]), refs[blocks:]
    att_ref, cache_ref, late_ref, keys, values, raw, weight_ref, normed, mixed, bias, sems = refs
    tokens = emb_ref.shape[0]
    step = tokens // 2
    group = q_heads // kv_heads
    _, count, rows, cols = raw.shape
    copies = block_copies(spots_ref, sources, raw, sems, pl.ds(0, cols))
    for copy in copies:
        copy.start()
    for r in range(0, tokens, step):
        x = emb_ref[r : r + step, :].astype(F32)
        scale = lax.rsqrt(jnp.mean(x * x, axis=-1, keepdims=True) + norm_eps)
        normed[r : r + step, :] = (x * scale * gain_ref[...]).astype(BF)
    bias[...] = bias_of(start_ref, tenant_ref, 0, step, step)
    for copy in copies:
        copy.wait()
    narrow, wide = spread_ref.shape
    target = 0
    for part in range(2):
        for b in range(cols // narrow):
            piece = raw[part, :, :, b * narrow : (b + 1) * narrow].reshape(count * rows, narrow)
            weight_ref[:, target : target + wide] = jnp.dot(
                piece, spread_ref[...], preferred_element_type=F32
            ).astype(BF)
            target += wide

    def turned(x):
        return (x * cos_ref[...] + pltpu.roll(x, 64, 1) * sin_ref[...]).astype(BF)

    def project(first, heads):
        return jnp.dot(
            normed[...],
            weight_ref[:, first * LANES : (first + heads) * LANES],
            preferred_element_type=F32,
        )

    k_all = project(q_heads, kv_heads)
    for h in range(kv_heads):
        keys[:, h * LANES : (h + 1) * LANES] = turned(k_all[:, h * LANES : (h + 1) * LANES])
    values[...] = project(q_heads + kv_heads, kv_heads).astype(BF)
    for kv in range(kv_heads):
        lanes = slice(kv * LANES, (kv + 1) * LANES)
        q_all = project(kv * group, group)
        for g in range(group):
            h = kv * group + g
            head = slice(h * LANES, (h + 1) * LANES)
            q = turned(q_all[:, g * LANES : (g + 1) * LANES])
            late_ref[:, head] = q[step:, :]
            mixed[:, head] = attend_head(
                q[:step, :], keys[:step, lanes], values[:step, lanes], bias[...]
            )
    att_ref[...] = packed(mixed[...], pack_ref)
    cache_ref[0] = packed(keys[...], pack_ref)
    cache_ref[1] = packed(values[...], pack_ref)


def late_kernel(
    q_heads, kv_heads, start_ref, tenant_ref, q_ref, keys, values, pack_ref, att_ref, mixed, bias
):
    step = q_ref.shape[0]
    seen = keys.shape[0]
    group = q_heads // kv_heads
    bias[...] = bias_of(start_ref, tenant_ref, seen - step, step, seen)
    for h in range(q_heads):
        head = slice(h * LANES, (h + 1) * LANES)
        lanes = slice(h // group * LANES, (h // group + 1) * LANES)
        mixed[:, head] = attend_head(q_ref[:, head], keys[:, lanes], values[:, lanes], bias[...])
    att_ref[...] = packed(mixed[...], pack_ref)


def block_list(refs):
    blocks = []
    for ref in refs:
        blocks += [ref] if len(ref.shape) == 2 else [ref.at[i] for i in range(ref.shape[0])]
    return blocks


def block_copies(spots_ref, sources, target, sems, cols):
    return [
        pltpu.make_async_copy(
            source.at[:, cols], target.at[spots_ref[0, s], spots_ref[1, s]], sems.at[s]
        )
        for s, source in enumerate(sources)
    ]


def attention_early(
    spots, starts, tenants, embedded, gain, cosine, sine, spread, blocks, cols, q_heads, kv_heads
):
    tokens, width = embedded.shape
    rows = blocks[0].shape[0]
    total = spots.shape[1]
    wide = 2 * cols // spread.shape[0] * spread.shape[1]
    step = tokens // 2
    return pl.pallas_call(
        functools.partial(project_kernel, q_heads, kv_heads, len(blocks)),
        out_shape=(
            jax.ShapeDtypeStruct((step, q_heads * HEAD_DIM), BF),
            jax.ShapeDtypeStruct((2, tokens, kv_heads * HEAD_DIM), BF),
            jax.ShapeDtypeStruct((step, q_heads * LANES), BF),
            jax.ShapeDtypeStruct((tokens, kv_heads * LANES), BF),
            jax.ShapeDtypeStruct((tokens, kv_heads * LANES), BF),
        ),
        in_specs=[pl.BlockSpec(memory_space=pltpu.SMEM)] * 3
        + in_vmem(6)
        + [pl.BlockSpec(memory_space=pl.ANY)] * len(blocks),
        out_specs=tuple(in_vmem(5)),
        scratch_shapes=[
            pltpu.VMEM((2, total // 2, rows, cols), BF),
            pltpu.VMEM((width, wide), BF),
            pltpu.VMEM((tokens, width), BF),
            pltpu.VMEM((step, q_heads * LANES), BF),
            pltpu.VMEM((step, step), F32),
            pltpu.SemaphoreType.DMA((total,)),
        ],
        compiler_params=params(),
        name="attention_early",
        cost_estimate=pl.CostEstimate(
            flops=2 * tokens * width * wide + 2 * width * wide * spread.shape[0],
            bytes_accessed=4 * width * wide + 6 * embedded.size,
            transcendentals=q_heads * step * step,
        ),
    )(spots, starts, tenants, embedded, gain, cosine, sine, spread, spread.T, *blocks)


def attention_late(starts, tenants, queries, keys, values, pack, q_heads, kv_heads):
    step, tokens = queries.shape[0], keys.shape[0]
    return pl.pallas_call(
        functools.partial(late_kernel, q_heads, kv_heads),
        out_shape=jax.ShapeDtypeStruct((step, q_heads * HEAD_DIM), BF),
        in_specs=[pl.BlockSpec(memory_space=pltpu.SMEM)] * 2 + in_vmem(4),
        out_specs=pl.BlockSpec(memory_space=pltpu.VMEM),
        scratch_shapes=[
            pltpu.VMEM((step, q_heads * LANES), BF),
            pltpu.VMEM((step, tokens), F32),
        ],
        compiler_params=params(),
        name="attention_late",
        cost_estimate=pl.CostEstimate(
            flops=4 * q_heads * step * tokens * LANES,
            bytes_accessed=8 * keys.size,
            transcendentals=q_heads * step * tokens,
        ),
    )(starts, tenants, queries, keys, values, pack)


def ffn_kernel(
    blocks,
    first_col,
    spots_ref,
    core_ref,
    emb_ref,
    own_ref,
    other_ref,
    w_own_ref,
    w_first_ref,
    w_second_ref,
    gain_ref,
    down_ref,
    *refs,
):
    sources, refs = block_list(refs[:blocks]), refs[blocks:]
    res_ref, part_ref, buf, down_buf, normed, total, sems, down_sems = refs
    _, _, count, rows, wide = buf.shape
    width = count * rows
    steps = down_ref.shape[0] // wide

    def copies(j):
        slot = j % 2
        made = block_copies(
            spots_ref, sources, buf.at[slot], sems.at[slot], pl.ds(first_col + j * wide, wide)
        )
        made.append(
            pltpu.make_async_copy(
                down_ref.at[pl.ds(j * wide, wide), :], down_buf.at[slot], down_sems.at[slot]
            )
        )
        return made

    pending = copies(0)
    for copy in pending:
        copy.start()
    depth = w_first_ref.shape[0]
    core = core_ref[0]
    first = pl.ds(pl.multiple_of(core * depth, LANES), depth)
    second = pl.ds(pl.multiple_of((1 - core) * depth, LANES), depth)
    x = (
        emb_ref[...].astype(F32)
        + jnp.dot(own_ref[...], w_own_ref[...], preferred_element_type=F32)
        + jnp.dot(other_ref[:, first], w_first_ref[...], preferred_element_type=F32)
        + jnp.dot(other_ref[:, second], w_second_ref[...], preferred_element_type=F32)
    )
    res_ref[...] = x
    scale = lax.rsqrt(jnp.mean(x * x, axis=-1, keepdims=True) + norm_eps)
    normed[...] = (x * scale * gain_ref[...]).astype(BF)
    for j in range(steps):
        current, slot = pending, j % 2
        if j + 1 < steps:
            pending = copies(j + 1)
            for copy in pending:
                copy.start()
        for copy in current:
            copy.wait()
        gate = jnp.dot(normed[...], buf[slot, 0].reshape(width, wide), preferred_element_type=F32)
        up = jnp.dot(normed[...], buf[slot, 1].reshape(width, wide), preferred_element_type=F32)
        hidden = (gate / (1.0 + jnp.exp(-gate)) * up).astype(BF)
        term = jnp.dot(hidden, down_buf[slot], preferred_element_type=F32)
        if j == 0:
            total[...] = term
        elif j + 1 < steps:
            total[...] += term
        else:
            part_ref[...] = (total[...] + term).astype(BF)


def ffn_part(
    spots, core, embedded, own, other, w_own, w_first, w_second, gain, down, blocks, first_col
):
    tokens, width = embedded.shape
    rows = blocks[0].shape[0]
    total = spots.shape[1]
    ff_half = down.shape[0]
    wide = min(512, ff_half)
    return pl.pallas_call(
        functools.partial(ffn_kernel, len(blocks), first_col),
        out_shape=(
            jax.ShapeDtypeStruct((tokens, width), F32),
            jax.ShapeDtypeStruct((tokens, width), BF),
        ),
        in_specs=[pl.BlockSpec(memory_space=pltpu.SMEM)] * 2
        + in_vmem(7)
        + [pl.BlockSpec(memory_space=pl.ANY)] * (1 + len(blocks)),
        out_specs=tuple(in_vmem(2)),
        scratch_shapes=[
            pltpu.VMEM((2, 2, total // 2, rows, wide), BF),
            pltpu.VMEM((2, wide, width), BF),
            pltpu.VMEM((tokens, width), BF),
            pltpu.VMEM((tokens, width), F32),
            pltpu.SemaphoreType.DMA((2, total)),
            pltpu.SemaphoreType.DMA((2,)),
        ],
        compiler_params=params(),
        name="ffn_part",
        cost_estimate=pl.CostEstimate(
            flops=2 * tokens * width * (3 * ff_half + 2 * w_own.shape[0]),
            bytes_accessed=6 * width * ff_half + 4 * w_own.size,
            transcendentals=tokens * ff_half,
        ),
    )(spots, core, embedded, own, other, w_own, w_first, w_second, gain, down, *blocks)


def per_device(
    token_ids,
    prompt_lengths,
    tenant_ids,
    embed_table,
    attention_gain,
    qkv_weight,
    out_weight,
    ffn_gain,
    gate_up_weight,
    down_weight,
):
    tp_count = lax.axis_size("tp")
    tp_index = lax.axis_index("tp")
    group_count = lax.axis_size("req")
    req_index = lax.axis_index("req")
    tokens = token_ids.shape[0]
    looked = tokens // tp_count
    own_rows, width = embed_table.shape
    capacity = max(2, 2 * looked // group_count)
    q_half = out_weight.shape[0]
    ff_half = down_weight.shape[0]
    q_full = q_half * tp_count
    kv_half = (qkv_weight.shape[1] - q_full) // (2 * tp_count)
    kv_full = kv_half * tp_count
    ff_full = ff_half * tp_count
    chips = group_count // 2
    core = req_index % 2
    chip = req_index // 2
    core_swap = [(i, i ^ 1) for i in range(group_count)]
    order, ring_pairs = chip_ring(chips)

    my_ids = lax.dynamic_slice_in_dim(token_ids, tp_index * looked, looked)
    owner_of = my_ids // own_rows
    row_in_range = my_ids - owner_of * own_rows
    earlier = jnp.arange(looked)[None, :] < jnp.arange(looked)[:, None]
    same = (owner_of[:, None] == owner_of[None, :]) & earlier
    place = owner_of * capacity + jnp.sum(same.astype(jnp.int32), axis=1)
    slots = jnp.arange(group_count * capacity, dtype=jnp.int32)
    chosen = place[None, :] == slots[:, None]
    requests = jnp.sum(jnp.where(chosen, row_in_range[None, :] + 1, 0), axis=1) - 1
    lengths = prompt_lengths[0]
    starts = jnp.stack([jnp.sum(lengths[:i]) for i in range(lengths.shape[0])]).astype(jnp.int32)
    offset = token_offsets(starts, tokens)
    lane = jnp.arange(LANES, dtype=jnp.int32)
    frequency = rope_base ** (-2.0 * (lane % 64).astype(F32) / HEAD_DIM)
    angles = offset.astype(F32)[:, None] * frequency[None, :]
    cosine = jnp.cos(angles)
    sine = jnp.where(lane < 64, -1.0, 1.0)[None, :] * jnp.sin(angles)

    asked = lax.all_to_all(
        requests.reshape(group_count, capacity), "req", split_axis=0, concat_axis=0, tiled=True
    ).reshape(-1)

    q_parts = ((0, q_half),)
    kv_parts = ((q_full, kv_half), (q_full + kv_full, kv_half))

    def columns(half, part):
        pieces = [
            lax.dynamic_slice_in_dim(qkv_weight, base + half * size, size, axis=1)
            for base, size in (q_parts, kv_parts)[part]
        ]
        pieces.append(
            lax.dynamic_slice_in_dim(
                gate_up_weight, part * ff_full + half * ff_half, ff_half, axis=1
            )
        )
        return jnp.concatenate([piece.astype(BF) for piece in pieces], axis=1)

    def chip_block(parts):
        kept = jnp.where(core == 0, parts[0], parts[1])
        moved = lax.ppermute(jnp.where(core == 0, parts[1], parts[0]), "req", core_swap)
        return jnp.concatenate(
            [jnp.where(core == 0, kept, moved), jnp.where(core == 0, moved, kept)], axis=0
        )

    own_ring = [chip_block([columns(tp_index, part) for part in range(2)])]
    away = jnp.stack([columns(1 - tp_index, part) for part in range(2)])
    came = lax.ppermute(away, "tp", PAIR)
    other_ring = [chip_block([came[part] for part in range(2)])]

    steps = jnp.arange(chips, dtype=jnp.int32)
    here = jnp.where(chip % 2 == 0, chip // 2, chips - 1 - chip // 2)

    def source_chip(position):
        position = position % chips
        return jnp.where(position < (chips + 1) // 2, 2 * position, 2 * (chips - 1 - position) + 1)

    up_chip, down_chip = source_chip(here - steps), source_chip(here + steps)
    mine = jnp.where(core == 0, up_chip, down_chip)
    theirs = jnp.where(core == 0, down_chip, up_chip)
    own_row, other_row = tp_index * chips, (1 - tp_index) * chips
    spots = jnp.stack(
        [
            jnp.repeat(jnp.stack([core, 1 - core]), 2 * chips),
            jnp.concatenate(
                [own_row + mine, other_row + mine, own_row + theirs, other_row + theirs]
            ),
        ]
    ).astype(jnp.int32)

    asked = after(asked, cosine, sine)
    pick_rows = (asked[:, None] == jnp.arange(own_rows, dtype=jnp.int32)[None, :]).astype(BF)
    found_rows = jnp.dot(pick_rows, embed_table, preferred_element_type=F32).astype(BF)
    returned = lax.all_to_all(
        found_rows.reshape(group_count, capacity, width),
        "req",
        split_axis=0,
        concat_axis=0,
        tiled=True,
    ).reshape(group_count * capacity, width)
    pick_mine = (place[:, None] == slots[None, :]).astype(BF)
    embedded_own = jnp.dot(pick_mine, returned, preferred_element_type=F32).astype(BF)
    embedded_other = lax.ppermute(embedded_own, "tp", PAIR)
    embedded = [
        jnp.where(tp_index == 0, embedded_own, embedded_other),
        jnp.where(tp_index == 0, embedded_other, embedded_own),
    ]

    out_rows = q_half // 2
    out_first = lax.ppermute(
        lax.dynamic_slice_in_dim(out_weight, core * out_rows, out_rows), "tp", PAIR
    )
    out_second = lax.ppermute(out_first, "req", core_swap)

    def swapped(blocks):
        return lax.ppermute(jnp.stack(blocks), "req", core_swap)

    cut = (chips + 2) // 2
    for i in range(chips - 1):
        ready = {2: (embedded_own,), 4: (embedded_other, out_second)}.get(i, ())
        own_ring = ring_more(own_ring, 1, ring_pairs, *ready)
        other_ring = ring_more(other_ring, 1, ring_pairs, *ready)
    blocks = [
        *own_ring,
        *other_ring,
        swapped(own_ring[:cut]),
        swapped(own_ring[cut:]),
        swapped(other_ring[:cut]),
        swapped(other_ring[cut:]),
    ]

    kv_local = kv_half // HEAD_DIM
    spread = spread_columns(kv_local)
    pack = spread.T
    q_local = q_half // HEAD_DIM
    early, kv_cache, queries, keys, values = attention_early(
        spots,
        starts,
        tenant_ids[0],
        jnp.concatenate(embedded, axis=0),
        attention_gain[None, :],
        cosine,
        sine,
        spread,
        blocks,
        q_half,
        q_local,
        kv_local,
    )
    late = attention_late(starts, tenant_ids[0], queries, keys, values, pack, q_local, kv_local)
    finals = []
    for start, attended in zip(embedded, (early, late)):
        residual, part = ffn_part(
            spots,
            core[None],
            start,
            attended,
            lax.ppermute(attended, "tp", PAIR),
            out_weight,
            out_first,
            out_second,
            ffn_gain[None, :],
            down_weight,
            blocks,
            q_half,
        )
        total = part.astype(F32) + lax.ppermute(part, "tp", PAIR).astype(F32)
        finals.append((residual + total).astype(BF))
    return (jnp.concatenate(finals, axis=0), kv_cache)


def solution(mesh):
    return jax.shard_map(
        per_device,
        mesh=mesh,
        in_specs=(
            P("req"),
            P("req", None),
            P("req", None),
            P("req", None),
            P(),
            P(("tp", "req"), None),
            P("tp", None),
            P(),
            P(("tp", "req"), None),
            P("tp", None),
        ),
        out_specs=(P("req", None), P(None, "req", "tp")),
        check_vma=False,
    )
```

```python
import functools
import math

import jax
import jax.numpy as jnp
from jax import lax
from jax.experimental import pallas as pl
from jax.experimental.pallas import tpu as pltpu
from jax.sharding import PartitionSpec as P

HEAD_DIM = 96
HALF = HEAD_DIM // 2
LANES = 128

rope_base = 100000.0
norm_eps = 1e-05

BF = jnp.bfloat16
F32 = jnp.float32
PAIR = [(0, 1), (1, 0)]


def token_offsets(lengths, row_count):
    positions = jnp.arange(row_count, dtype=jnp.int32)
    offset, start = positions, 0
    for i in range(1, lengths.shape[0]):
        start = start + lengths[i - 1]
        offset = jnp.where(positions >= start, positions - start, offset)
    return offset


def after(value, *others):
    return lax.optimization_barrier((value, *others))[0]


def chip_ring(chips):
    order = list(range(0, chips, 2)) + list(range(chips - 1 - chips % 2, 0, -2))
    following = {order[i]: order[(i + 1) % chips] for i in range(chips)}
    pairs = [(2 * c, 2 * d) for c, d in following.items()]
    pairs += [(2 * d + 1, 2 * c + 1) for c, d in following.items()]
    return order, pairs


def ring_more(blocks, count, pairs, *ready):
    blocks = list(blocks)
    for i in range(count):
        last = after(blocks[-1], *ready) if ready and i == 0 else blocks[-1]
        blocks.append(lax.ppermute(last, "req", pairs))
    return blocks


def in_vmem(count):
    return [pl.BlockSpec(memory_space=pltpu.VMEM)] * count


def params(mebibytes):
    return pltpu.CompilerParams(vmem_limit_bytes=mebibytes * 1024 * 1024)


def spread_columns(heads):
    column = jnp.arange(heads * HEAD_DIM, dtype=jnp.int32)
    within = column % HEAD_DIM
    target = column // HEAD_DIM * LANES + jnp.where(within < HALF, within, within + 64 - HALF)
    return (target[:, None] == jnp.arange(heads * LANES, dtype=jnp.int32)[None, :]).astype(BF)


def tenant_at(length_ref, tenant_ref, positions):
    tenant, start = jnp.full(positions.shape, tenant_ref[0], jnp.int32), 0
    for i in range(1, tenant_ref.shape[0]):
        start = start + length_ref[i - 1]
        tenant = jnp.where(positions >= start, tenant_ref[i], tenant)
    return tenant


def bias_of(length_ref, tenant_ref, first, count, seen):
    row = lax.broadcasted_iota(jnp.int32, (count, seen), 0) + first
    col = lax.broadcasted_iota(jnp.int32, (count, seen), 1)
    query_tenant = tenant_at(
        length_ref, tenant_ref, lax.broadcasted_iota(jnp.int32, (count, 1), 0) + first
    )
    key_tenant = tenant_at(length_ref, tenant_ref, lax.broadcasted_iota(jnp.int32, (1, seen), 1))
    return jnp.where((col <= row) & (query_tenant == key_tenant), 0.0, -1e30)


def attend_head(q, keys, values, bias):
    scores = lax.dot_general(q, keys, (((1,), (1,)), ((), ())), preferred_element_type=F32) + bias
    top = jnp.max(scores, axis=-1, keepdims=True)
    expo = jnp.exp2((scores - top) * (HEAD_DIM**-0.5 * math.log2(math.e)))
    total = jnp.sum(expo, axis=-1, keepdims=True)
    out = jnp.dot(expo.astype(BF), values, preferred_element_type=F32)
    return (out / total).astype(BF)


def packed(x, pack_ref):
    wide = pack_ref.shape[0]
    return jnp.concatenate(
        [
            jnp.dot(x[:, b : b + wide], pack_ref[...], preferred_element_type=F32).astype(BF)
            for b in range(0, x.shape[1], wide)
        ],
        axis=1,
    )


def project_kernel(
    q_heads,
    kv_heads,
    blocks,
    spots_ref,
    length_ref,
    tenant_ref,
    half_ref,
    own_ref,
    other_ref,
    gain_ref,
    cos_ref,
    low_ref,
    high_ref,
    spread_ref,
    pack_ref,
    *refs,
):
    sources, refs = block_list(refs[:blocks]), refs[blocks:]
    att_ref, cache_ref, late_ref, keys, values, raw, normed, mixed, bias, sems = refs
    step = own_ref.shape[0]
    group = q_heads // kv_heads
    _, count, rows, cols = raw.shape
    copies = block_copies(spots_ref, sources, raw, sems, pl.ds(0, cols))
    for copy in copies:
        copy.start()
    for half, ref in ((half_ref[0], own_ref), (1 - half_ref[0], other_ref)):
        x = ref[...].astype(F32)
        scale = lax.rsqrt(jnp.mean(x * x, axis=-1, keepdims=True) + norm_eps)
        place = pl.ds(pl.multiple_of(half * step, step), step)
        normed[place, :] = (x * scale * gain_ref[...]).astype(BF)
    bias[...] = bias_of(length_ref, tenant_ref, 0, step, step)
    for copy in copies:
        copy.wait()
    narrow, wide = spread_ref.shape

    def turned(x):
        return (
            x * cos_ref[...]
            + pltpu.roll(x, narrow - HALF, 1) * low_ref[...]
            + pltpu.roll(x, HALF, 1) * high_ref[...]
        ).astype(BF)

    def spread(x):
        return jnp.dot(x, spread_ref[...], preferred_element_type=F32).astype(BF)

    def project(part):
        return jnp.dot(
            normed[...], raw[part].reshape(count * rows, cols), preferred_element_type=F32
        )

    key_value = project(1)
    key_heads = turned(key_value[:, :narrow])
    value_heads = key_value[:, narrow:].astype(BF)
    cache_ref[0] = key_heads
    cache_ref[1] = value_heads
    keys[...] = spread(key_heads)
    values[...] = spread(value_heads)
    query = project(0)
    for b in range(cols // narrow):
        q_wide = spread(turned(query[:, b * narrow : (b + 1) * narrow]))
        late_ref[:, b * wide : (b + 1) * wide] = q_wide[step:, :]
        for g in range(wide // LANES):
            h = b * (wide // LANES) + g
            lanes = slice(h // group * LANES, (h // group + 1) * LANES)
            mixed[:, h * LANES : (h + 1) * LANES] = attend_head(
                q_wide[:step, g * LANES : (g + 1) * LANES],
                keys[:step, lanes],
                values[:step, lanes],
                bias[...],
            )
    att_ref[...] = packed(mixed[...], pack_ref)


def late_kernel(
    q_heads, kv_heads, length_ref, tenant_ref, q_ref, keys, values, pack_ref, att_ref, mixed, bias
):
    step = q_ref.shape[0]
    seen = keys.shape[0]
    group = q_heads // kv_heads
    bias[...] = bias_of(length_ref, tenant_ref, seen - step, step, seen)
    for h in range(q_heads):
        head = slice(h * LANES, (h + 1) * LANES)
        lanes = slice(h // group * LANES, (h // group + 1) * LANES)
        mixed[:, head] = attend_head(q_ref[:, head], keys[:, lanes], values[:, lanes], bias[...])
    att_ref[...] = packed(mixed[...], pack_ref)


def block_list(refs):
    blocks = []
    for ref in refs:
        blocks += [ref] if len(ref.shape) == 2 else [ref.at[i] for i in range(ref.shape[0])]
    return blocks


def block_copies(spots_ref, sources, target, sems, cols):
    return [
        pltpu.make_async_copy(
            source.at[:, cols], target.at[spots_ref[0, s], spots_ref[1, s]], sems.at[s]
        )
        for s, source in enumerate(sources)
    ]


def attention_early(
    spots, lengths, tenants, half, own, other, gain, tables, spread, blocks, cols, q_heads, kv_heads
):
    step, width = own.shape
    tokens = 2 * step
    rows = blocks[0].shape[0]
    total = spots.shape[1]
    return pl.pallas_call(
        functools.partial(project_kernel, q_heads, kv_heads, len(blocks)),
        out_shape=(
            jax.ShapeDtypeStruct((step, q_heads * HEAD_DIM), BF),
            jax.ShapeDtypeStruct((2, tokens, kv_heads * HEAD_DIM), BF),
            jax.ShapeDtypeStruct((step, q_heads * LANES), BF),
            jax.ShapeDtypeStruct((tokens, kv_heads * LANES), BF),
            jax.ShapeDtypeStruct((tokens, kv_heads * LANES), BF),
        ),
        in_specs=[pl.BlockSpec(memory_space=pltpu.SMEM)] * 4
        + in_vmem(8)
        + [pl.BlockSpec(memory_space=pl.ANY)] * len(blocks),
        out_specs=tuple(in_vmem(5)),
        scratch_shapes=[
            pltpu.VMEM((2, total // 2, rows, cols), BF),
            pltpu.VMEM((tokens, width), BF),
            pltpu.VMEM((step, q_heads * LANES), BF),
            pltpu.VMEM((step, step), F32),
            pltpu.SemaphoreType.DMA((total,)),
        ],
        compiler_params=params(48),
        name="attention_early",
        cost_estimate=pl.CostEstimate(
            flops=4 * tokens * width * cols,
            bytes_accessed=4 * width * cols + 12 * own.size,
            transcendentals=q_heads * step * step,
        ),
    )(spots, lengths, tenants, half, own, other, gain, *tables, spread, spread.T, *blocks)


def attention_late(lengths, tenants, queries, keys, values, pack, q_heads, kv_heads):
    step, tokens = queries.shape[0], keys.shape[0]
    return pl.pallas_call(
        functools.partial(late_kernel, q_heads, kv_heads),
        out_shape=jax.ShapeDtypeStruct((step, q_heads * HEAD_DIM), BF),
        in_specs=[pl.BlockSpec(memory_space=pltpu.SMEM)] * 2 + in_vmem(4),
        out_specs=pl.BlockSpec(memory_space=pltpu.VMEM),
        scratch_shapes=[
            pltpu.VMEM((step, q_heads * LANES), BF),
            pltpu.VMEM((step, tokens), F32),
        ],
        compiler_params=params(48),
        name="attention_late",
        cost_estimate=pl.CostEstimate(
            flops=4 * q_heads * step * tokens * LANES,
            bytes_accessed=8 * keys.size,
            transcendentals=q_heads * step * tokens,
        ),
    )(lengths, tenants, queries, keys, values, pack)


def ffn_kernel(
    blocks,
    first_col,
    spots_ref,
    side_ref,
    emb_own_ref,
    emb_other_ref,
    own_ref,
    other_ref,
    w_own_ref,
    w_first_ref,
    w_second_ref,
    gain_ref,
    down_ref,
    *refs,
):
    sources, refs = block_list(refs[:blocks]), refs[blocks:]
    res_ref, part_ref, buf, down_buf, normed, total, sems, down_sems = refs
    _, _, count, rows, wide = buf.shape
    width = count * rows
    steps = down_ref.shape[0] // wide

    def copies(j):
        slot = j % 2
        made = block_copies(
            spots_ref, sources, buf.at[slot], sems.at[slot], pl.ds(first_col + j * wide, wide)
        )
        made.append(
            pltpu.make_async_copy(
                down_ref.at[pl.ds(j * wide, wide), :], down_buf.at[slot], down_sems.at[slot]
            )
        )
        return made

    pending = copies(0)
    for copy in pending:
        copy.start()
    depth = w_first_ref.shape[0]
    core = side_ref[0]
    first = pl.ds(pl.multiple_of(core * depth, LANES), depth)
    second = pl.ds(pl.multiple_of((1 - core) * depth, LANES), depth)
    embedded = jnp.where(side_ref[1] == 1, emb_own_ref[...], emb_other_ref[...])
    x = (
        embedded.astype(F32)
        + jnp.dot(own_ref[...], w_own_ref[...], preferred_element_type=F32)
        + jnp.dot(other_ref[:, first], w_first_ref[...], preferred_element_type=F32)
        + jnp.dot(other_ref[:, second], w_second_ref[...], preferred_element_type=F32)
    )
    res_ref[...] = x
    scale = lax.rsqrt(jnp.mean(x * x, axis=-1, keepdims=True) + norm_eps)
    normed[...] = (x * scale * gain_ref[...]).astype(BF)
    for j in range(steps):
        current, slot = pending, j % 2
        if j + 1 < steps:
            pending = copies(j + 1)
            for copy in pending:
                copy.start()
        for copy in current:
            copy.wait()
        gate = jnp.dot(normed[...], buf[slot, 0].reshape(width, wide), preferred_element_type=F32)
        up = jnp.dot(normed[...], buf[slot, 1].reshape(width, wide), preferred_element_type=F32)
        hidden = (gate / (1.0 + jnp.exp(-gate)) * up).astype(BF)
        term = jnp.dot(hidden, down_buf[slot], preferred_element_type=F32)
        if j == 0:
            total[...] = term
        elif j + 1 < steps:
            total[...] += term
        else:
            part_ref[...] = (total[...] + term).astype(BF)


def ffn_part(
    spots, side, embedded, own, other, w_own, w_first, w_second, gain, down, blocks, first_col
):
    tokens, width = embedded[0].shape
    rows = blocks[0].shape[0]
    total = spots.shape[1]
    ff_half = down.shape[0]
    wide = min(512, ff_half)
    return pl.pallas_call(
        functools.partial(ffn_kernel, len(blocks), first_col),
        out_shape=(
            jax.ShapeDtypeStruct((tokens, width), F32),
            jax.ShapeDtypeStruct((tokens, width), BF),
        ),
        in_specs=[pl.BlockSpec(memory_space=pltpu.SMEM)] * 2
        + in_vmem(8)
        + [pl.BlockSpec(memory_space=pl.ANY)] * (1 + len(blocks)),
        out_specs=tuple(in_vmem(2)),
        scratch_shapes=[
            pltpu.VMEM((2, 2, total // 2, rows, wide), BF),
            pltpu.VMEM((2, wide, width), BF),
            pltpu.VMEM((tokens, width), BF),
            pltpu.VMEM((tokens, width), F32),
            pltpu.SemaphoreType.DMA((2, total)),
            pltpu.SemaphoreType.DMA((2,)),
        ],
        compiler_params=params(48),
        name="ffn_part",
        cost_estimate=pl.CostEstimate(
            flops=2 * tokens * width * (3 * ff_half + 2 * w_own.shape[0]),
            bytes_accessed=6 * width * ff_half + 4 * w_own.size,
            transcendentals=tokens * ff_half,
        ),
    )(spots, side, *embedded, own, other, w_own, w_first, w_second, gain, down, *blocks)


def per_device(
    token_ids,
    prompt_lengths,
    tenant_ids,
    embed_table,
    attention_gain,
    qkv_weight,
    out_weight,
    ffn_gain,
    gate_up_weight,
    down_weight,
):
    tp_count = lax.axis_size("tp")
    tp_index = lax.axis_index("tp")
    group_count = lax.axis_size("req")
    req_index = lax.axis_index("req")
    tokens = token_ids.shape[0]
    looked = tokens // tp_count
    own_rows, width = embed_table.shape
    capacity = max(2, 2 * looked // group_count)
    q_half = out_weight.shape[0]
    ff_half = down_weight.shape[0]
    q_full = q_half * tp_count
    kv_half = (qkv_weight.shape[1] - q_full) // (2 * tp_count)
    kv_full = kv_half * tp_count
    ff_full = ff_half * tp_count
    chips = group_count // 2
    core = req_index % 2
    chip = req_index // 2
    core_swap = [(i, i ^ 1) for i in range(group_count)]
    order, ring_pairs = chip_ring(chips)

    my_ids = lax.dynamic_slice_in_dim(token_ids, tp_index * looked, looked)
    owner_of = my_ids // own_rows
    row_in_range = my_ids - owner_of * own_rows
    earlier = jnp.arange(looked)[None, :] < jnp.arange(looked)[:, None]
    same = (owner_of[:, None] == owner_of[None, :]) & earlier
    place = owner_of * capacity + jnp.sum(same.astype(jnp.int32), axis=1)
    slots = jnp.arange(group_count * capacity, dtype=jnp.int32)
    chosen = place[None, :] == slots[:, None]
    requests = jnp.sum(jnp.where(chosen, row_in_range[None, :] + 1, 0), axis=1) - 1
    asked = lax.all_to_all(
        requests.reshape(group_count, capacity), "req", split_axis=0, concat_axis=0, tiled=True
    ).reshape(-1)

    pick_rows = (asked[:, None] == jnp.arange(own_rows, dtype=jnp.int32)[None, :]).astype(BF)
    found_rows = jnp.dot(pick_rows, embed_table, preferred_element_type=F32).astype(BF)
    returned = lax.all_to_all(
        found_rows.reshape(group_count, capacity, width),
        "req",
        split_axis=0,
        concat_axis=0,
        tiled=True,
    ).reshape(group_count * capacity, width)
    lengths = prompt_lengths[0]
    kv_local = kv_half // HEAD_DIM
    lane = jnp.arange(kv_half, dtype=jnp.int32) % HEAD_DIM
    frequency = rope_base ** (-2.0 * (lane % HALF).astype(F32) / HEAD_DIM)
    offset = token_offsets(after(lengths, found_rows), tokens)
    angles = offset.astype(F32)[:, None] * frequency[None, :]
    sine = jnp.sin(angles)
    low = lane < HALF
    tables = (jnp.cos(angles), jnp.where(low, -sine, 0.0), jnp.where(low, 0.0, sine))

    q_parts = ((0, q_half),)
    kv_parts = ((q_full, kv_half), (q_full + kv_full, kv_half))

    def columns(half, part):
        pieces = [
            lax.dynamic_slice_in_dim(qkv_weight, base + half * size, size, axis=1)
            for base, size in (q_parts, kv_parts)[part]
        ]
        pieces.append(
            lax.dynamic_slice_in_dim(
                gate_up_weight, part * ff_full + half * ff_half, ff_half, axis=1
            )
        )
        return after(jnp.concatenate([piece.astype(BF) for piece in pieces], axis=1), *tables)

    def chip_block(parts):
        kept = jnp.where(core == 0, parts[0], parts[1])
        moved = lax.ppermute(jnp.where(core == 0, parts[1], parts[0]), "req", core_swap)
        return jnp.concatenate(
            [jnp.where(core == 0, kept, moved), jnp.where(core == 0, moved, kept)], axis=0
        )

    own_ring = [chip_block([columns(tp_index, part) for part in range(2)])]
    away = jnp.stack([columns(1 - tp_index, part) for part in range(2)])
    came = lax.ppermute(away, "tp", PAIR)
    other_ring = [chip_block([came[part] for part in range(2)])]

    steps = jnp.arange(chips, dtype=jnp.int32)
    here = jnp.where(chip % 2 == 0, chip // 2, chips - 1 - chip // 2)

    def source_chip(position):
        position = position % chips
        return jnp.where(position < (chips + 1) // 2, 2 * position, 2 * (chips - 1 - position) + 1)

    up_chip, down_chip = source_chip(here - steps), source_chip(here + steps)
    mine = jnp.where(core == 0, up_chip, down_chip)
    theirs = jnp.where(core == 0, down_chip, up_chip)
    own_row, other_row = tp_index * chips, (1 - tp_index) * chips
    spots = jnp.stack(
        [
            jnp.repeat(jnp.stack([core, 1 - core]), 2 * chips),
            jnp.concatenate(
                [own_row + mine, other_row + mine, own_row + theirs, other_row + theirs]
            ),
        ]
    ).astype(jnp.int32)

    pick_mine = (place[:, None] == slots[None, :]).astype(BF)
    embedded_own = jnp.dot(pick_mine, returned, preferred_element_type=F32).astype(BF)
    embedded_other = lax.ppermute(embedded_own, "tp", PAIR)

    out_rows = q_half // 2
    out_first = lax.ppermute(
        after(lax.dynamic_slice_in_dim(out_weight, core * out_rows, out_rows), came), "tp", PAIR
    )
    out_second = lax.ppermute(out_first, "req", core_swap)

    def swapped(blocks):
        sent = blocks[0] if len(blocks) == 1 else jnp.stack(blocks)
        return lax.ppermute(sent, "req", core_swap)

    cut = (chips + 2) // 2
    for i in range(chips - 1):
        ready = {2: (embedded_own,), chips - 3: (embedded_other, out_second)}.get(i, ())
        own_ring = ring_more(own_ring, 1, ring_pairs, other_ring[max(i - 1, 0)], *ready)
        other_ring = ring_more(other_ring, 1, ring_pairs, own_ring[i])
    blocks = [
        *own_ring,
        *other_ring,
        swapped(own_ring[:cut]),
        swapped(own_ring[cut:-1]),
        swapped(own_ring[-1:]),
        swapped(other_ring[:cut]),
        swapped(other_ring[cut:-1]),
        swapped(other_ring[-1:]),
    ]

    spread = spread_columns(kv_local)
    pack = spread.T
    q_local = q_half // HEAD_DIM
    early, kv_cache, queries, keys, values = attention_early(
        spots,
        lengths,
        tenant_ids[0],
        tp_index[None],
        embedded_own,
        embedded_other,
        attention_gain[None, :],
        tables,
        spread,
        blocks,
        q_half,
        q_local,
        kv_local,
    )
    late = attention_late(lengths, tenant_ids[0], queries, keys, values, pack, q_local, kv_local)
    finals = []
    for half, attended in enumerate((early, late)):
        residual, part = ffn_part(
            spots,
            jnp.stack([core, (tp_index == half).astype(jnp.int32)]),
            (embedded_own, embedded_other),
            attended,
            lax.ppermute(attended, "tp", PAIR),
            out_weight,
            out_first,
            out_second,
            ffn_gain[None, :],
            down_weight,
            blocks,
            q_half,
        )
        total = part.astype(F32) + lax.ppermute(part, "tp", PAIR).astype(F32)
        finals.append((residual + total).astype(BF))
    return (jnp.concatenate(finals, axis=0), kv_cache)


def solution(mesh):
    return jax.shard_map(
        per_device,
        mesh=mesh,
        in_specs=(
            P("req"),
            P("req", None),
            P("req", None),
            P("req", None),
            P(),
            P(("tp", "req"), None),
            P("tp", None),
            P(),
            P(("tp", "req"), None),
            P("tp", None),
        ),
        out_specs=(P("req", None), P(None, "req", "tp")),
        check_vma=False,
    )
```

```python
import functools
import math

import jax
import jax.numpy as jnp
from jax import lax
from jax.experimental import pallas as pl
from jax.experimental.pallas import tpu as pltpu
from jax.sharding import PartitionSpec as P

HEAD_DIM = 96
HALF = HEAD_DIM // 2
LANES = 128

rope_base = 100000.0
norm_eps = 1e-05

BF = jnp.bfloat16
F32 = jnp.float32
PAIR = [(0, 1), (1, 0)]


def token_offsets(lengths, row_count):
    positions = jnp.arange(row_count, dtype=jnp.int32)
    offset, start = positions, 0
    for i in range(1, lengths.shape[0]):
        start = start + lengths[i - 1]
        offset = jnp.where(positions >= start, positions - start, offset)
    return offset


def after(value, *others):
    return lax.optimization_barrier((value, *others))[0]


def chip_ring(chips):
    order = list(range(0, chips, 2)) + list(range(chips - 1 - chips % 2, 0, -2))
    following = {order[i]: order[(i + 1) % chips] for i in range(chips)}
    pairs = [(2 * c, 2 * d) for c, d in following.items()]
    pairs += [(2 * d + 1, 2 * c + 1) for c, d in following.items()]
    return order, pairs


def ring_more(blocks, count, pairs, *ready):
    blocks = list(blocks)
    for i in range(count):
        last = after(blocks[-1], *ready) if ready and i == 0 else blocks[-1]
        blocks.append(lax.ppermute(last, "req", pairs))
    return blocks


def in_vmem(count):
    return [pl.BlockSpec(memory_space=pltpu.VMEM)] * count


def params(mebibytes):
    return pltpu.CompilerParams(vmem_limit_bytes=mebibytes * 1024 * 1024)


def spread_columns(heads):
    column = jnp.arange(heads * HEAD_DIM, dtype=jnp.int32)
    within = column % HEAD_DIM
    target = column // HEAD_DIM * LANES + jnp.where(within < HALF, within, within + 64 - HALF)
    return (target[:, None] == jnp.arange(heads * LANES, dtype=jnp.int32)[None, :]).astype(BF)


def tenant_at(length_ref, tenant_ref, positions):
    tenant, start = jnp.full(positions.shape, tenant_ref[0], jnp.int32), 0
    for i in range(1, tenant_ref.shape[0]):
        start = start + length_ref[i - 1]
        tenant = jnp.where(positions >= start, tenant_ref[i], tenant)
    return tenant


def bias_of(length_ref, tenant_ref, first, count, seen):
    row = lax.broadcasted_iota(jnp.int32, (count, seen), 0) + first
    col = lax.broadcasted_iota(jnp.int32, (count, seen), 1)
    query_tenant = tenant_at(
        length_ref, tenant_ref, lax.broadcasted_iota(jnp.int32, (count, 1), 0) + first
    )
    key_tenant = tenant_at(length_ref, tenant_ref, lax.broadcasted_iota(jnp.int32, (1, seen), 1))
    return jnp.where((col <= row) & (query_tenant == key_tenant), 0.0, -1e30)


def attend_head(q, keys, values, bias):
    scores = lax.dot_general(q, keys, (((1,), (1,)), ((), ())), preferred_element_type=F32) + bias
    top = jnp.max(scores, axis=-1, keepdims=True)
    expo = jnp.exp2((scores - top) * (HEAD_DIM**-0.5 * math.log2(math.e)))
    total = jnp.sum(expo, axis=-1, keepdims=True)
    out = jnp.dot(expo.astype(BF), values, preferred_element_type=F32)
    return (out / total).astype(BF)


def packed(x, pack_ref):
    wide = pack_ref.shape[0]
    return jnp.concatenate(
        [
            jnp.dot(x[:, b : b + wide], pack_ref[...], preferred_element_type=F32).astype(BF)
            for b in range(0, x.shape[1], wide)
        ],
        axis=1,
    )


def project_kernel(
    q_heads,
    kv_heads,
    blocks,
    spots_ref,
    length_ref,
    tenant_ref,
    half_ref,
    own_ref,
    other_ref,
    gain_ref,
    cos_ref,
    low_ref,
    high_ref,
    spread_ref,
    pack_ref,
    *refs,
):
    sources, refs = block_list(refs[:blocks]), refs[blocks:]
    att_ref, cache_ref, late_ref, keys, values, raw, normed, mixed, bias, sems = refs
    step = own_ref.shape[0]
    group = q_heads // kv_heads
    _, count, rows, cols = raw.shape
    copies = block_copies(spots_ref, sources, raw, sems, pl.ds(0, cols))
    for copy in copies:
        copy.start()
    for half, ref in ((half_ref[0], own_ref), (1 - half_ref[0], other_ref)):
        x = ref[...].astype(F32)
        scale = lax.rsqrt(jnp.mean(x * x, axis=-1, keepdims=True) + norm_eps)
        place = pl.ds(pl.multiple_of(half * step, step), step)
        normed[place, :] = (x * scale * gain_ref[...]).astype(BF)
    bias[...] = bias_of(length_ref, tenant_ref, 0, step, step)
    for copy in copies:
        copy.wait()
    narrow, wide = spread_ref.shape

    def turned(x):
        return (
            x * cos_ref[...]
            + pltpu.roll(x, narrow - HALF, 1) * low_ref[...]
            + pltpu.roll(x, HALF, 1) * high_ref[...]
        ).astype(BF)

    def spread(x):
        return jnp.dot(x, spread_ref[...], preferred_element_type=F32).astype(BF)

    def project(part):
        return jnp.dot(
            normed[...], raw[part].reshape(count * rows, cols), preferred_element_type=F32
        )

    key_value = project(1)
    key_heads = turned(key_value[:, :narrow])
    value_heads = key_value[:, narrow:].astype(BF)
    cache_ref[0] = key_heads
    cache_ref[1] = value_heads
    keys[...] = spread(key_heads)
    values[...] = spread(value_heads)
    query = project(0)
    for b in range(cols // narrow):
        q_wide = spread(turned(query[:, b * narrow : (b + 1) * narrow]))
        late_ref[:, b * wide : (b + 1) * wide] = q_wide[step:, :]
        for g in range(wide // LANES):
            h = b * (wide // LANES) + g
            lanes = slice(h // group * LANES, (h // group + 1) * LANES)
            mixed[:, h * LANES : (h + 1) * LANES] = attend_head(
                q_wide[:step, g * LANES : (g + 1) * LANES],
                keys[:step, lanes],
                values[:step, lanes],
                bias[...],
            )
    att_ref[...] = packed(mixed[...], pack_ref)


def late_kernel(
    q_heads, kv_heads, length_ref, tenant_ref, q_ref, keys, values, pack_ref, att_ref, mixed, bias
):
    step = q_ref.shape[0]
    seen = keys.shape[0]
    group = q_heads // kv_heads
    bias[...] = bias_of(length_ref, tenant_ref, seen - step, step, seen)
    for h in range(q_heads):
        head = slice(h * LANES, (h + 1) * LANES)
        lanes = slice(h // group * LANES, (h // group + 1) * LANES)
        mixed[:, head] = attend_head(q_ref[:, head], keys[:, lanes], values[:, lanes], bias[...])
    att_ref[...] = packed(mixed[...], pack_ref)


def block_list(refs):
    blocks = []
    for ref in refs:
        blocks += [ref] if len(ref.shape) == 2 else [ref.at[i] for i in range(ref.shape[0])]
    return blocks


def block_copies(spots_ref, sources, target, sems, cols):
    return [
        pltpu.make_async_copy(
            source.at[:, cols], target.at[spots_ref[0, s], spots_ref[1, s]], sems.at[s]
        )
        for s, source in enumerate(sources)
    ]


def attention_early(
    spots, lengths, tenants, half, own, other, gain, tables, spread, blocks, cols, q_heads, kv_heads
):
    step, width = own.shape
    tokens = 2 * step
    rows = blocks[0].shape[0]
    total = spots.shape[1]
    return pl.pallas_call(
        functools.partial(project_kernel, q_heads, kv_heads, len(blocks)),
        out_shape=(
            jax.ShapeDtypeStruct((step, q_heads * HEAD_DIM), BF),
            jax.ShapeDtypeStruct((2, tokens, kv_heads * HEAD_DIM), BF),
            jax.ShapeDtypeStruct((step, q_heads * LANES), BF),
            jax.ShapeDtypeStruct((tokens, kv_heads * LANES), BF),
            jax.ShapeDtypeStruct((tokens, kv_heads * LANES), BF),
        ),
        in_specs=[pl.BlockSpec(memory_space=pltpu.SMEM)] * 4
        + in_vmem(8)
        + [pl.BlockSpec(memory_space=pl.ANY)] * len(blocks),
        out_specs=tuple(in_vmem(5)),
        scratch_shapes=[
            pltpu.VMEM((2, total // 2, rows, cols), BF),
            pltpu.VMEM((tokens, width), BF),
            pltpu.VMEM((step, q_heads * LANES), BF),
            pltpu.VMEM((step, step), F32),
            pltpu.SemaphoreType.DMA((total,)),
        ],
        compiler_params=params(52),
        name="attention_early",
        cost_estimate=pl.CostEstimate(
            flops=4 * tokens * width * cols,
            bytes_accessed=4 * width * cols + 12 * own.size,
            transcendentals=q_heads * step * step,
        ),
    )(spots, lengths, tenants, half, own, other, gain, *tables, spread, spread.T, *blocks)


def attention_late(lengths, tenants, queries, keys, values, pack, q_heads, kv_heads):
    step, tokens = queries.shape[0], keys.shape[0]
    return pl.pallas_call(
        functools.partial(late_kernel, q_heads, kv_heads),
        out_shape=jax.ShapeDtypeStruct((step, q_heads * HEAD_DIM), BF),
        in_specs=[pl.BlockSpec(memory_space=pltpu.SMEM)] * 2 + in_vmem(4),
        out_specs=pl.BlockSpec(memory_space=pltpu.VMEM),
        scratch_shapes=[
            pltpu.VMEM((step, q_heads * LANES), BF),
            pltpu.VMEM((step, tokens), F32),
        ],
        compiler_params=params(48),
        name="attention_late",
        cost_estimate=pl.CostEstimate(
            flops=4 * q_heads * step * tokens * LANES,
            bytes_accessed=8 * keys.size,
            transcendentals=q_heads * step * tokens,
        ),
    )(lengths, tenants, queries, keys, values, pack)


def ffn_kernel(
    blocks,
    first_col,
    spots_ref,
    side_ref,
    base_ref,
    other_ref,
    w_first_ref,
    w_second_ref,
    gain_ref,
    down_ref,
    *refs,
):
    sources, refs = block_list(refs[:blocks]), refs[blocks:]
    res_ref, part_ref, buf, down_buf, normed, total, sems, down_sems = refs
    _, _, count, rows, wide = buf.shape
    width = count * rows
    steps = down_ref.shape[0] // wide

    def copies(j):
        slot = j % 2
        made = block_copies(
            spots_ref, sources, buf.at[slot], sems.at[slot], pl.ds(first_col + j * wide, wide)
        )
        made.append(
            pltpu.make_async_copy(
                down_ref.at[pl.ds(j * wide, wide), :], down_buf.at[slot], down_sems.at[slot]
            )
        )
        return made

    pending = copies(0)
    for copy in pending:
        copy.start()
    depth = w_first_ref.shape[0]
    core = side_ref[0]
    first = pl.ds(pl.multiple_of(core * depth, LANES), depth)
    second = pl.ds(pl.multiple_of((1 - core) * depth, LANES), depth)
    x = (
        base_ref[...]
        + jnp.dot(other_ref[:, first], w_first_ref[...], preferred_element_type=F32)
        + jnp.dot(other_ref[:, second], w_second_ref[...], preferred_element_type=F32)
    )
    res_ref[...] = x
    scale = lax.rsqrt(jnp.mean(x * x, axis=-1, keepdims=True) + norm_eps)
    normed[...] = (x * scale * gain_ref[...]).astype(BF)
    for j in range(steps):
        current, slot = pending, j % 2
        if j + 1 < steps:
            pending = copies(j + 1)
            for copy in pending:
                copy.start()
        for copy in current:
            copy.wait()
        gate = jnp.dot(normed[...], buf[slot, 0].reshape(width, wide), preferred_element_type=F32)
        up = jnp.dot(normed[...], buf[slot, 1].reshape(width, wide), preferred_element_type=F32)
        hidden = (gate / (1.0 + jnp.exp(-gate)) * up).astype(BF)
        term = jnp.dot(hidden, down_buf[slot], preferred_element_type=F32)
        if j == 0:
            total[...] = term
        elif j + 1 < steps:
            total[...] += term
        else:
            part_ref[...] = (total[...] + term).astype(BF)


def ffn_part(spots, side, base, other, w_first, w_second, gain, down, blocks, first_col):
    tokens, width = base.shape
    rows = blocks[0].shape[0]
    total = spots.shape[1]
    ff_half = down.shape[0]
    wide = min(512, ff_half)
    return pl.pallas_call(
        functools.partial(ffn_kernel, len(blocks), first_col),
        out_shape=(
            jax.ShapeDtypeStruct((tokens, width), F32),
            jax.ShapeDtypeStruct((tokens, width), BF),
        ),
        in_specs=[pl.BlockSpec(memory_space=pltpu.SMEM)] * 2
        + in_vmem(5)
        + [pl.BlockSpec(memory_space=pl.ANY)] * (1 + len(blocks)),
        out_specs=tuple(in_vmem(2)),
        scratch_shapes=[
            pltpu.VMEM((2, 2, total // 2, rows, wide), BF),
            pltpu.VMEM((2, wide, width), BF),
            pltpu.VMEM((tokens, width), BF),
            pltpu.VMEM((tokens, width), F32),
            pltpu.SemaphoreType.DMA((2, total)),
            pltpu.SemaphoreType.DMA((2,)),
        ],
        compiler_params=params(48),
        name="ffn_part",
        cost_estimate=pl.CostEstimate(
            flops=2 * tokens * width * (3 * ff_half + 2 * w_first.shape[0]),
            bytes_accessed=6 * width * ff_half + 4 * w_first.size,
            transcendentals=tokens * ff_half,
        ),
    )(spots, side, base, other, w_first, w_second, gain, down, *blocks)


def per_device(
    token_ids,
    prompt_lengths,
    tenant_ids,
    embed_table,
    attention_gain,
    qkv_weight,
    out_weight,
    ffn_gain,
    gate_up_weight,
    down_weight,
):
    tp_count = lax.axis_size("tp")
    tp_index = lax.axis_index("tp")
    group_count = lax.axis_size("req")
    req_index = lax.axis_index("req")
    tokens = token_ids.shape[0]
    looked = tokens // tp_count
    own_rows, width = embed_table.shape
    capacity = max(2, 2 * looked // group_count)
    q_half = out_weight.shape[0]
    ff_half = down_weight.shape[0]
    q_full = q_half * tp_count
    kv_half = (qkv_weight.shape[1] - q_full) // (2 * tp_count)
    kv_full = kv_half * tp_count
    ff_full = ff_half * tp_count
    chips = group_count // 2
    core = req_index % 2
    chip = req_index // 2
    core_swap = [(i, i ^ 1) for i in range(group_count)]
    order, ring_pairs = chip_ring(chips)

    my_ids = lax.dynamic_slice_in_dim(token_ids, tp_index * looked, looked)
    owner_of = my_ids // own_rows
    row_in_range = my_ids - owner_of * own_rows
    earlier = jnp.arange(looked)[None, :] < jnp.arange(looked)[:, None]
    same = (owner_of[:, None] == owner_of[None, :]) & earlier
    place = owner_of * capacity + jnp.sum(same.astype(jnp.int32), axis=1)
    slots = jnp.arange(group_count * capacity, dtype=jnp.int32)
    chosen = place[None, :] == slots[:, None]
    requests = jnp.sum(jnp.where(chosen, row_in_range[None, :] + 1, 0), axis=1) - 1
    asked = lax.all_to_all(
        requests.reshape(group_count, capacity), "req", split_axis=0, concat_axis=0, tiled=True
    ).reshape(-1)

    pick_rows = (asked[:, None] == jnp.arange(own_rows, dtype=jnp.int32)[None, :]).astype(BF)
    found_rows = jnp.dot(pick_rows, embed_table, preferred_element_type=F32).astype(BF)
    returned = lax.all_to_all(
        found_rows.reshape(group_count, capacity, width),
        "req",
        split_axis=0,
        concat_axis=0,
        tiled=True,
    ).reshape(group_count * capacity, width)
    lengths = prompt_lengths[0]
    kv_local = kv_half // HEAD_DIM
    lane = jnp.arange(kv_half, dtype=jnp.int32) % HEAD_DIM
    frequency = rope_base ** (-2.0 * (lane % HALF).astype(F32) / HEAD_DIM)
    offset = token_offsets(after(lengths, found_rows), tokens)
    angles = offset.astype(F32)[:, None] * frequency[None, :]
    sine = jnp.sin(angles)
    low = lane < HALF
    tables = (jnp.cos(angles), jnp.where(low, -sine, 0.0), jnp.where(low, 0.0, sine))

    q_parts = ((0, q_half),)
    kv_parts = ((q_full, kv_half), (q_full + kv_full, kv_half))

    def columns(half, part):
        pieces = [
            lax.dynamic_slice_in_dim(qkv_weight, base + half * size, size, axis=1)
            for base, size in (q_parts, kv_parts)[part]
        ]
        pieces.append(
            lax.dynamic_slice_in_dim(
                gate_up_weight, part * ff_full + half * ff_half, ff_half, axis=1
            )
        )
        return after(jnp.concatenate([piece.astype(BF) for piece in pieces], axis=1), *tables)

    def chip_block(parts):
        kept = jnp.where(core == 0, parts[0], parts[1])
        moved = lax.ppermute(jnp.where(core == 0, parts[1], parts[0]), "req", core_swap)
        return jnp.concatenate(
            [jnp.where(core == 0, kept, moved), jnp.where(core == 0, moved, kept)], axis=0
        )

    own_ring = [chip_block([columns(tp_index, part) for part in range(2)])]
    away = jnp.stack([columns(1 - tp_index, part) for part in range(2)])
    came = lax.ppermute(away, "tp", PAIR)
    other_ring = [chip_block([came[part] for part in range(2)])]

    steps = jnp.arange(chips, dtype=jnp.int32)
    here = jnp.where(chip % 2 == 0, chip // 2, chips - 1 - chip // 2)

    def source_chip(position):
        position = position % chips
        return jnp.where(position < (chips + 1) // 2, 2 * position, 2 * (chips - 1 - position) + 1)

    up_chip, down_chip = source_chip(here - steps), source_chip(here + steps)
    mine = jnp.where(core == 0, up_chip, down_chip)
    theirs = jnp.where(core == 0, down_chip, up_chip)
    own_row, other_row = tp_index * chips, (1 - tp_index) * chips
    spots = jnp.stack(
        [
            jnp.repeat(jnp.stack([core, 1 - core]), 2 * chips),
            jnp.concatenate(
                [own_row + mine, other_row + mine, own_row + theirs, other_row + theirs]
            ),
        ]
    ).astype(jnp.int32)

    pick_mine = (place[:, None] == slots[None, :]).astype(BF)
    embedded_own = jnp.dot(pick_mine, returned, preferred_element_type=F32).astype(BF)
    embedded_other = lax.ppermute(embedded_own, "tp", PAIR)

    out_rows = q_half // 2
    out_first = lax.ppermute(
        after(lax.dynamic_slice_in_dim(out_weight, core * out_rows, out_rows), came), "tp", PAIR
    )
    def swapped(blocks):
        sent = blocks[0] if len(blocks) == 1 else jnp.stack(blocks)
        return lax.ppermute(sent, "req", core_swap)

    cut = (chips + 2) // 2
    for i in range(chips - 1):
        ready = {2: (embedded_own,), chips - 3: (embedded_other,)}.get(i, ())
        own_ring = ring_more(own_ring, 1, ring_pairs, other_ring[max(i - 1, 0)], *ready)
        other_ring = ring_more(other_ring, 1, ring_pairs, own_ring[i])
    out_second = lax.ppermute(after(out_first, own_ring[chips - 2]), "req", core_swap)
    blocks = [
        *own_ring,
        *other_ring,
        swapped(own_ring[:cut]),
        swapped(own_ring[cut:-1]),
        swapped(own_ring[-1:]),
        swapped(other_ring[:cut]),
        swapped(other_ring[cut:-1]),
        swapped(other_ring[-1:]),
    ]

    spread = spread_columns(kv_local)
    pack = spread.T
    q_local = q_half // HEAD_DIM
    early, kv_cache, queries, keys, values = attention_early(
        spots,
        lengths,
        tenant_ids[0],
        tp_index[None],
        embedded_own,
        embedded_other,
        attention_gain[None, :],
        tables,
        spread,
        blocks,
        q_half,
        q_local,
        kv_local,
    )
    late = attention_late(lengths, tenant_ids[0], queries, keys, values, pack, q_local, kv_local)
    finals = []
    for half, attended in enumerate((early, late)):
        start = jnp.where(tp_index == half, embedded_own, embedded_other).astype(F32)
        residual, part = ffn_part(
            spots,
            core[None],
            start + jnp.dot(attended, out_weight, preferred_element_type=F32),
            lax.ppermute(attended, "tp", PAIR),
            out_first,
            out_second,
            ffn_gain[None, :],
            down_weight,
            blocks,
            q_half,
        )
        total = part.astype(F32) + lax.ppermute(part, "tp", PAIR).astype(F32)
        finals.append((residual + total).astype(BF))
    return (jnp.concatenate(finals, axis=0), kv_cache)


def solution(mesh):
    return jax.shard_map(
        per_device,
        mesh=mesh,
        in_specs=(
            P("req"),
            P("req", None),
            P("req", None),
            P("req", None),
            P(),
            P(("tp", "req"), None),
            P("tp", None),
            P(),
            P(("tp", "req"), None),
            P("tp", None),
        ),
        out_specs=(P("req", None), P(None, "req", "tp")),
        check_vma=False,
    )
```

```python
import functools
import math

import jax
import jax.numpy as jnp
from jax import lax
from jax.experimental import pallas as pl
from jax.experimental.pallas import tpu as pltpu
from jax.sharding import PartitionSpec as P

HEAD_DIM = 96
HALF = HEAD_DIM // 2
LANES = 128

rope_base = 100000.0
norm_eps = 1e-05

BF = jnp.bfloat16
F32 = jnp.float32
PAIR = [(0, 1), (1, 0)]


def token_offsets(lengths, row_count):
    positions = jnp.arange(row_count, dtype=jnp.int32)
    offset, start = positions, 0
    for i in range(1, lengths.shape[0]):
        start = start + lengths[i - 1]
        offset = jnp.where(positions >= start, positions - start, offset)
    return offset


def after(value, *others):
    return lax.optimization_barrier((value, *others))[0]


def chip_ring(chips):
    order = list(range(0, chips, 2)) + list(range(chips - 1 - chips % 2, 0, -2))
    following = {order[i]: order[(i + 1) % chips] for i in range(chips)}
    pairs = [(2 * c, 2 * d) for c, d in following.items()]
    pairs += [(2 * d + 1, 2 * c + 1) for c, d in following.items()]
    return order, pairs


def ring_more(blocks, count, pairs, *ready):
    blocks = list(blocks)
    for i in range(count):
        last = after(blocks[-1], *ready) if ready and i == 0 else blocks[-1]
        blocks.append(lax.ppermute(last, "req", pairs))
    return blocks


def in_vmem(count):
    return [pl.BlockSpec(memory_space=pltpu.VMEM)] * count


def params(mebibytes):
    return pltpu.CompilerParams(vmem_limit_bytes=mebibytes * 1024 * 1024)


def spread_columns(heads):
    column = jnp.arange(heads * HEAD_DIM, dtype=jnp.int32)
    within = column % HEAD_DIM
    target = column // HEAD_DIM * LANES + jnp.where(within < HALF, within, within + 64 - HALF)
    return (target[:, None] == jnp.arange(heads * LANES, dtype=jnp.int32)[None, :]).astype(BF)


def tenant_at(length_ref, tenant_ref, positions):
    tenant, start = jnp.full(positions.shape, tenant_ref[0], jnp.int32), 0
    for i in range(1, tenant_ref.shape[0]):
        start = start + length_ref[i - 1]
        tenant = jnp.where(positions >= start, tenant_ref[i], tenant)
    return tenant


def bias_of(length_ref, tenant_ref, first, count, seen):
    row = lax.broadcasted_iota(jnp.int32, (count, seen), 0) + first
    col = lax.broadcasted_iota(jnp.int32, (count, seen), 1)
    query_tenant = tenant_at(
        length_ref, tenant_ref, lax.broadcasted_iota(jnp.int32, (count, 1), 0) + first
    )
    key_tenant = tenant_at(length_ref, tenant_ref, lax.broadcasted_iota(jnp.int32, (1, seen), 1))
    return jnp.where((col <= row) & (query_tenant == key_tenant), 0.0, -1e30)


def attend_head(q, keys, values, bias):
    scores = lax.dot_general(q, keys, (((1,), (1,)), ((), ())), preferred_element_type=F32) + bias
    top = jnp.max(scores, axis=-1, keepdims=True)
    expo = jnp.exp2((scores - top) * (HEAD_DIM**-0.5 * math.log2(math.e)))
    total = jnp.sum(expo, axis=-1, keepdims=True)
    out = jnp.dot(expo.astype(BF), values, preferred_element_type=F32)
    return (out / total).astype(BF)


def packed(x, pack_ref):
    wide = pack_ref.shape[0]
    return jnp.concatenate(
        [
            jnp.dot(x[:, b : b + wide], pack_ref[...], preferred_element_type=F32).astype(BF)
            for b in range(0, x.shape[1], wide)
        ],
        axis=1,
    )


def project_kernel(
    q_heads,
    kv_heads,
    blocks,
    spots_ref,
    length_ref,
    tenant_ref,
    half_ref,
    own_ref,
    other_ref,
    gain_ref,
    cos_ref,
    low_ref,
    high_ref,
    spread_ref,
    pack_ref,
    *refs,
):
    sources, refs = block_list(refs[:blocks]), refs[blocks:]
    att_ref, cache_ref, late_ref, keys, values, raw, normed, mixed, bias, sems = refs
    step = own_ref.shape[0]
    group = q_heads // kv_heads
    _, count, rows, cols = raw.shape
    copies = block_copies(spots_ref, sources, raw, sems, pl.ds(0, cols))
    for copy in copies:
        copy.start()
    for half, ref in ((half_ref[0], own_ref), (1 - half_ref[0], other_ref)):
        x = ref[...].astype(F32)
        scale = lax.rsqrt(jnp.mean(x * x, axis=-1, keepdims=True) + norm_eps)
        place = pl.ds(pl.multiple_of(half * step, step), step)
        normed[place, :] = (x * scale * gain_ref[...]).astype(BF)
    bias[...] = bias_of(length_ref, tenant_ref, 0, step, step)
    for copy in copies:
        copy.wait()
    narrow, wide = spread_ref.shape

    def turned(x):
        return (
            x * cos_ref[...]
            + pltpu.roll(x, narrow - HALF, 1) * low_ref[...]
            + pltpu.roll(x, HALF, 1) * high_ref[...]
        ).astype(BF)

    def spread(x):
        return jnp.dot(x, spread_ref[...], preferred_element_type=F32).astype(BF)

    def project(part):
        return jnp.dot(
            normed[...], raw[part].reshape(count * rows, cols), preferred_element_type=F32
        )

    key_value = project(1)
    key_heads = turned(key_value[:, :narrow])
    value_heads = key_value[:, narrow:].astype(BF)
    cache_ref[0] = key_heads
    cache_ref[1] = value_heads
    keys[...] = spread(key_heads)
    values[...] = spread(value_heads)
    query = project(0)
    for b in range(cols // narrow):
        q_wide = spread(turned(query[:, b * narrow : (b + 1) * narrow]))
        late_ref[:, b * wide : (b + 1) * wide] = q_wide[step:, :]
        for g in range(wide // LANES):
            h = b * (wide // LANES) + g
            lanes = slice(h // group * LANES, (h // group + 1) * LANES)
            mixed[:, h * LANES : (h + 1) * LANES] = attend_head(
                q_wide[:step, g * LANES : (g + 1) * LANES],
                keys[:step, lanes],
                values[:step, lanes],
                bias[...],
            )
    att_ref[...] = packed(mixed[...], pack_ref)


def late_kernel(
    q_heads, kv_heads, length_ref, tenant_ref, q_ref, keys, values, pack_ref, att_ref, mixed, bias
):
    step = q_ref.shape[0]
    seen = keys.shape[0]
    group = q_heads // kv_heads
    bias[...] = bias_of(length_ref, tenant_ref, seen - step, step, seen)
    for h in range(q_heads):
        head = slice(h * LANES, (h + 1) * LANES)
        lanes = slice(h // group * LANES, (h // group + 1) * LANES)
        mixed[:, head] = attend_head(q_ref[:, head], keys[:, lanes], values[:, lanes], bias[...])
    att_ref[...] = packed(mixed[...], pack_ref)


def block_list(refs):
    blocks = []
    for ref in refs:
        blocks += [ref] if len(ref.shape) == 2 else [ref.at[i] for i in range(ref.shape[0])]
    return blocks


def block_copies(spots_ref, sources, target, sems, cols):
    return [
        pltpu.make_async_copy(
            source.at[:, cols], target.at[spots_ref[0, s], spots_ref[1, s]], sems.at[s]
        )
        for s, source in enumerate(sources)
    ]


def attention_early(
    spots, lengths, tenants, half, own, other, gain, tables, spread, blocks, cols, q_heads, kv_heads
):
    step, width = own.shape
    tokens = 2 * step
    rows = blocks[0].shape[0]
    total = spots.shape[1]
    return pl.pallas_call(
        functools.partial(project_kernel, q_heads, kv_heads, len(blocks)),
        out_shape=(
            jax.ShapeDtypeStruct((step, q_heads * HEAD_DIM), BF),
            jax.ShapeDtypeStruct((2, tokens, kv_heads * HEAD_DIM), BF),
            jax.ShapeDtypeStruct((step, q_heads * LANES), BF),
            jax.ShapeDtypeStruct((tokens, kv_heads * LANES), BF),
            jax.ShapeDtypeStruct((tokens, kv_heads * LANES), BF),
        ),
        in_specs=[pl.BlockSpec(memory_space=pltpu.SMEM)] * 4
        + in_vmem(8)
        + [pl.BlockSpec(memory_space=pl.ANY)] * len(blocks),
        out_specs=tuple(in_vmem(5)),
        scratch_shapes=[
            pltpu.VMEM((2, total // 2, rows, cols), BF),
            pltpu.VMEM((tokens, width), BF),
            pltpu.VMEM((step, q_heads * LANES), BF),
            pltpu.VMEM((step, step), F32),
            pltpu.SemaphoreType.DMA((total,)),
        ],
        compiler_params=params(52),
        name="attention_early",
        cost_estimate=pl.CostEstimate(
            flops=4 * tokens * width * cols,
            bytes_accessed=4 * width * cols + 12 * own.size,
            transcendentals=q_heads * step * step,
        ),
    )(spots, lengths, tenants, half, own, other, gain, *tables, spread, spread.T, *blocks)


def attention_late(lengths, tenants, queries, keys, values, pack, q_heads, kv_heads):
    step, tokens = queries.shape[0], keys.shape[0]
    return pl.pallas_call(
        functools.partial(late_kernel, q_heads, kv_heads),
        out_shape=jax.ShapeDtypeStruct((step, q_heads * HEAD_DIM), BF),
        in_specs=[pl.BlockSpec(memory_space=pltpu.SMEM)] * 2 + in_vmem(4),
        out_specs=pl.BlockSpec(memory_space=pltpu.VMEM),
        scratch_shapes=[
            pltpu.VMEM((step, q_heads * LANES), BF),
            pltpu.VMEM((step, tokens), F32),
        ],
        compiler_params=params(48),
        name="attention_late",
        cost_estimate=pl.CostEstimate(
            flops=4 * q_heads * step * tokens * LANES,
            bytes_accessed=8 * keys.size,
            transcendentals=q_heads * step * tokens,
        ),
    )(lengths, tenants, queries, keys, values, pack)


def ffn_kernel(
    blocks,
    first_col,
    spots_ref,
    side_ref,
    base_ref,
    other_ref,
    w_first_ref,
    w_second_ref,
    gain_ref,
    down_ref,
    *refs,
):
    sources, refs = block_list(refs[:blocks]), refs[blocks:]
    res_ref, part_ref, buf, down_buf, normed, total, sems, down_sems = refs
    _, _, count, rows, wide = buf.shape
    width = count * rows
    steps = down_ref.shape[0] // wide

    def copies(j):
        slot = j % 2
        made = block_copies(
            spots_ref, sources, buf.at[slot], sems.at[slot], pl.ds(first_col + j * wide, wide)
        )
        made.append(
            pltpu.make_async_copy(
                down_ref.at[pl.ds(j * wide, wide), :], down_buf.at[slot], down_sems.at[slot]
            )
        )
        return made

    pending = copies(0)
    for copy in pending:
        copy.start()
    depth = w_first_ref.shape[0]
    core = side_ref[0]
    first = pl.ds(pl.multiple_of(core * depth, LANES), depth)
    second = pl.ds(pl.multiple_of((1 - core) * depth, LANES), depth)
    x = (
        base_ref[...]
        + jnp.dot(other_ref[:, first], w_first_ref[...], preferred_element_type=F32)
        + jnp.dot(other_ref[:, second], w_second_ref[...], preferred_element_type=F32)
    )
    res_ref[...] = x
    scale = lax.rsqrt(jnp.mean(x * x, axis=-1, keepdims=True) + norm_eps)
    normed[...] = (x * scale * gain_ref[...]).astype(BF)
    for j in range(steps):
        current, slot = pending, j % 2
        if j + 1 < steps:
            pending = copies(j + 1)
            for copy in pending:
                copy.start()
        for copy in current:
            copy.wait()
        gate = jnp.dot(normed[...], buf[slot, 0].reshape(width, wide), preferred_element_type=F32)
        up = jnp.dot(normed[...], buf[slot, 1].reshape(width, wide), preferred_element_type=F32)
        hidden = (gate / (1.0 + jnp.exp(-gate)) * up).astype(BF)
        term = jnp.dot(hidden, down_buf[slot], preferred_element_type=F32)
        if j == 0:
            total[...] = term
        elif j + 1 < steps:
            total[...] += term
        else:
            part_ref[...] = (total[...] + term).astype(BF)


def ffn_part(spots, side, base, other, w_first, w_second, gain, down, blocks, first_col):
    tokens, width = base.shape
    rows = blocks[0].shape[0]
    total = spots.shape[1]
    ff_half = down.shape[0]
    wide = min(512, ff_half)
    return pl.pallas_call(
        functools.partial(ffn_kernel, len(blocks), first_col),
        out_shape=(
            jax.ShapeDtypeStruct((tokens, width), F32),
            jax.ShapeDtypeStruct((tokens, width), BF),
        ),
        in_specs=[pl.BlockSpec(memory_space=pltpu.SMEM)] * 2
        + in_vmem(5)
        + [pl.BlockSpec(memory_space=pl.ANY)] * (1 + len(blocks)),
        out_specs=tuple(in_vmem(2)),
        scratch_shapes=[
            pltpu.VMEM((2, 2, total // 2, rows, wide), BF),
            pltpu.VMEM((2, wide, width), BF),
            pltpu.VMEM((tokens, width), BF),
            pltpu.VMEM((tokens, width), F32),
            pltpu.SemaphoreType.DMA((2, total)),
            pltpu.SemaphoreType.DMA((2,)),
        ],
        compiler_params=params(48),
        name="ffn_part",
        cost_estimate=pl.CostEstimate(
            flops=2 * tokens * width * (3 * ff_half + 2 * w_first.shape[0]),
            bytes_accessed=6 * width * ff_half + 4 * w_first.size,
            transcendentals=tokens * ff_half,
        ),
    )(spots, side, base, other, w_first, w_second, gain, down, *blocks)


def per_device(
    token_ids,
    prompt_lengths,
    tenant_ids,
    embed_table,
    attention_gain,
    qkv_weight,
    out_weight,
    ffn_gain,
    gate_up_weight,
    down_weight,
):
    tp_count = lax.axis_size("tp")
    tp_index = lax.axis_index("tp")
    group_count = lax.axis_size("req")
    req_index = lax.axis_index("req")
    tokens = token_ids.shape[0]
    looked = tokens // tp_count
    own_rows, width = embed_table.shape
    capacity = max(2, 2 * looked // group_count)
    q_half = out_weight.shape[0]
    ff_half = down_weight.shape[0]
    q_full = q_half * tp_count
    kv_half = (qkv_weight.shape[1] - q_full) // (2 * tp_count)
    kv_full = kv_half * tp_count
    ff_full = ff_half * tp_count
    chips = group_count // 2
    core = req_index % 2
    chip = req_index // 2
    core_swap = [(i, i ^ 1) for i in range(group_count)]
    order, ring_pairs = chip_ring(chips)

    my_ids = lax.dynamic_slice_in_dim(token_ids, tp_index * looked, looked)
    owner_of = my_ids // own_rows
    row_in_range = my_ids - owner_of * own_rows
    earlier = jnp.arange(looked)[None, :] < jnp.arange(looked)[:, None]
    same = (owner_of[:, None] == owner_of[None, :]) & earlier
    place = owner_of * capacity + jnp.sum(same.astype(jnp.int32), axis=1)
    slots = jnp.arange(group_count * capacity, dtype=jnp.int32)
    chosen = place[None, :] == slots[:, None]
    requests = jnp.sum(jnp.where(chosen, row_in_range[None, :] + 1, 0), axis=1) - 1
    asked = lax.all_to_all(
        requests.reshape(group_count, capacity), "req", split_axis=0, concat_axis=0, tiled=True
    ).reshape(-1)

    pick_rows = (asked[:, None] == jnp.arange(own_rows, dtype=jnp.int32)[None, :]).astype(BF)
    found_rows = jnp.dot(pick_rows, embed_table, preferred_element_type=F32).astype(BF)
    returned = lax.all_to_all(
        found_rows.reshape(group_count, capacity, width),
        "req",
        split_axis=0,
        concat_axis=0,
        tiled=True,
    ).reshape(group_count * capacity, width)
    lengths = prompt_lengths[0]
    kv_local = kv_half // HEAD_DIM
    lane = jnp.arange(kv_half, dtype=jnp.int32) % HEAD_DIM
    frequency = rope_base ** (-2.0 * (lane % HALF).astype(F32) / HEAD_DIM)
    offset = token_offsets(after(lengths, found_rows), tokens)
    angles = offset.astype(F32)[:, None] * frequency[None, :]
    sine = jnp.sin(angles)
    low = lane < HALF
    tables = (jnp.cos(angles), jnp.where(low, -sine, 0.0), jnp.where(low, 0.0, sine))

    q_parts = ((0, q_half),)
    kv_parts = ((q_full, kv_half), (q_full + kv_full, kv_half))

    def columns(half, part):
        pieces = [
            lax.dynamic_slice_in_dim(qkv_weight, base + half * size, size, axis=1)
            for base, size in (q_parts, kv_parts)[part]
        ]
        pieces.append(
            lax.dynamic_slice_in_dim(
                gate_up_weight, part * ff_full + half * ff_half, ff_half, axis=1
            )
        )
        return after(jnp.concatenate([piece.astype(BF) for piece in pieces], axis=1), *tables)

    def chip_block(parts):
        kept = jnp.where(core == 0, parts[0], parts[1])
        moved = lax.ppermute(jnp.where(core == 0, parts[1], parts[0]), "req", core_swap)
        return jnp.concatenate(
            [jnp.where(core == 0, kept, moved), jnp.where(core == 0, moved, kept)], axis=0
        )

    own_ring = [chip_block([columns(tp_index, part) for part in range(2)])]
    away = jnp.stack([columns(1 - tp_index, part) for part in range(2)])
    came = lax.ppermute(away, "tp", PAIR)
    other_ring = [chip_block([came[part] for part in range(2)])]

    steps = jnp.arange(chips, dtype=jnp.int32)
    here = jnp.where(chip % 2 == 0, chip // 2, chips - 1 - chip // 2)

    def source_chip(position):
        position = position % chips
        return jnp.where(position < (chips + 1) // 2, 2 * position, 2 * (chips - 1 - position) + 1)

    up_chip, down_chip = source_chip(here - steps), source_chip(here + steps)
    mine = jnp.where(core == 0, up_chip, down_chip)
    theirs = jnp.where(core == 0, down_chip, up_chip)
    own_row, other_row = tp_index * chips, (1 - tp_index) * chips
    spots = jnp.stack(
        [
            jnp.repeat(jnp.stack([core, 1 - core]), 2 * chips),
            jnp.concatenate(
                [own_row + mine, other_row + mine, own_row + theirs, other_row + theirs]
            ),
        ]
    ).astype(jnp.int32)

    pick_mine = (place[:, None] == slots[None, :]).astype(BF)
    embedded_own = jnp.dot(pick_mine, returned, preferred_element_type=F32).astype(BF)
    embedded_other = lax.ppermute(embedded_own, "tp", PAIR)

    out_rows = q_half // 2
    out_first = lax.ppermute(
        after(lax.dynamic_slice_in_dim(out_weight, core * out_rows, out_rows), came), "tp", PAIR
    )
    def swapped(blocks):
        sent = blocks[0] if len(blocks) == 1 else jnp.stack(blocks)
        return lax.ppermute(sent, "req", core_swap)

    cut = (chips + 2) // 2
    for i in range(chips - 1):
        ready = {2: (embedded_own,), chips - 3: (embedded_other,)}.get(i, ())
        own_ring = ring_more(own_ring, 1, ring_pairs, other_ring[max(i - 1, 0)], *ready)
        other_ring = ring_more(other_ring, 1, ring_pairs, own_ring[i])
    out_second = lax.ppermute(after(out_first, own_ring[chips - 2]), "req", core_swap)
    blocks = [
        *own_ring,
        *other_ring,
        swapped(own_ring[:cut]),
        swapped(own_ring[cut:-1]),
        swapped(own_ring[-1:]),
        swapped(other_ring[:cut]),
        swapped(other_ring[cut:-1]),
        swapped(other_ring[-1:]),
    ]

    spread = spread_columns(kv_local)
    pack = spread.T
    q_local = q_half // HEAD_DIM
    early, kv_cache, queries, keys, values = attention_early(
        spots,
        lengths,
        tenant_ids[0],
        tp_index[None],
        embedded_own,
        embedded_other,
        attention_gain[None, :],
        tables,
        spread,
        blocks,
        q_half,
        q_local,
        kv_local,
    )
    early_other = lax.ppermute(early, "tp", PAIR)
    queries = after(queries, early_other)
    late = attention_late(lengths, tenant_ids[0], queries, keys, values, pack, q_local, kv_local)
    finals = []
    late_other = lax.ppermute(late, "tp", PAIR)
    sides = ((early, early_other), (late, late_other))
    for half, (attended, came_over) in enumerate(sides):
        start = jnp.where(tp_index == half, embedded_own, embedded_other).astype(F32)
        residual, part = ffn_part(
            spots,
            core[None],
            start + jnp.dot(attended, out_weight, preferred_element_type=F32),
            came_over,
            out_first,
            out_second,
            ffn_gain[None, :],
            down_weight,
            blocks,
            q_half,
        )
        total = part.astype(F32) + lax.ppermute(part, "tp", PAIR).astype(F32)
        finals.append((residual + total).astype(BF))
    return (jnp.concatenate(finals, axis=0), kv_cache)


def solution(mesh):
    return jax.shard_map(
        per_device,
        mesh=mesh,
        in_specs=(
            P("req"),
            P("req", None),
            P("req", None),
            P("req", None),
            P(),
            P(("tp", "req"), None),
            P("tp", None),
            P(),
            P(("tp", "req"), None),
            P("tp", None),
        ),
        out_specs=(P("req", None), P(None, "req", "tp")),
        check_vma=False,
    )
```

```python
import functools
import math

import jax
import jax.numpy as jnp
from jax import lax
from jax.experimental import pallas as pl
from jax.experimental.pallas import tpu as pltpu
from jax.sharding import PartitionSpec as P

HEAD_DIM = 96
HALF = HEAD_DIM // 2
LANES = 128

rope_base = 100000.0
norm_eps = 1e-05

BF = jnp.bfloat16
F32 = jnp.float32
PAIR = [(0, 1), (1, 0)]


def token_offsets(lengths, row_count):
    positions = jnp.arange(row_count, dtype=jnp.int32)
    offset, start = positions, 0
    for i in range(1, lengths.shape[0]):
        start = start + lengths[i - 1]
        offset = jnp.where(positions >= start, positions - start, offset)
    return offset


def after(value, *others):
    return lax.optimization_barrier((value, *others))[0]


def chip_ring(chips):
    order = list(range(0, chips, 2)) + list(range(chips - 1 - chips % 2, 0, -2))
    following = {order[i]: order[(i + 1) % chips] for i in range(chips)}
    pairs = [(2 * c, 2 * d) for c, d in following.items()]
    pairs += [(2 * d + 1, 2 * c + 1) for c, d in following.items()]
    return order, pairs


def ring_more(blocks, count, pairs, *ready):
    blocks = list(blocks)
    for i in range(count):
        last = after(blocks[-1], *ready) if ready and i == 0 else blocks[-1]
        blocks.append(lax.ppermute(last, "req", pairs))
    return blocks


def in_vmem(count):
    return [pl.BlockSpec(memory_space=pltpu.VMEM)] * count


def params(mebibytes):
    return pltpu.CompilerParams(vmem_limit_bytes=mebibytes * 1024 * 1024)


def spread_columns(heads):
    column = jnp.arange(heads * HEAD_DIM, dtype=jnp.int32)
    within = column % HEAD_DIM
    target = column // HEAD_DIM * LANES + jnp.where(within < HALF, within, within + 64 - HALF)
    return (target[:, None] == jnp.arange(heads * LANES, dtype=jnp.int32)[None, :]).astype(BF)


def tenant_at(length_ref, tenant_ref, positions):
    tenant, start = jnp.full(positions.shape, tenant_ref[0], jnp.int32), 0
    for i in range(1, tenant_ref.shape[0]):
        start = start + length_ref[i - 1]
        tenant = jnp.where(positions >= start, tenant_ref[i], tenant)
    return tenant


def bias_of(length_ref, tenant_ref, first, count, seen):
    row = lax.broadcasted_iota(jnp.int32, (count, seen), 0) + first
    col = lax.broadcasted_iota(jnp.int32, (count, seen), 1)
    query_tenant = tenant_at(
        length_ref, tenant_ref, lax.broadcasted_iota(jnp.int32, (count, 1), 0) + first
    )
    key_tenant = tenant_at(length_ref, tenant_ref, lax.broadcasted_iota(jnp.int32, (1, seen), 1))
    return jnp.where((col <= row) & (query_tenant == key_tenant), 0.0, -1e30)


def attend_head(q, keys, values, bias):
    scores = lax.dot_general(q, keys, (((1,), (1,)), ((), ())), preferred_element_type=F32) + bias
    top = jnp.max(scores, axis=-1, keepdims=True)
    expo = jnp.exp2((scores - top) * (HEAD_DIM**-0.5 * math.log2(math.e)))
    total = jnp.sum(expo, axis=-1, keepdims=True)
    out = jnp.dot(expo.astype(BF), values, preferred_element_type=F32)
    return (out / total).astype(BF)


def packed(x, pack_ref):
    wide = pack_ref.shape[0]
    return jnp.concatenate(
        [
            jnp.dot(x[:, b : b + wide], pack_ref[...], preferred_element_type=F32).astype(BF)
            for b in range(0, x.shape[1], wide)
        ],
        axis=1,
    )


def project_kernel(
    q_heads,
    kv_heads,
    blocks,
    spots_ref,
    length_ref,
    tenant_ref,
    half_ref,
    own_ref,
    other_ref,
    gain_ref,
    cos_ref,
    low_ref,
    high_ref,
    spread_ref,
    pack_ref,
    *refs,
):
    sources, refs = block_list(refs[:blocks]), refs[blocks:]
    att_ref, cache_ref, late_ref, keys, values, raw, normed, mixed, bias, sems = refs
    step = own_ref.shape[0]
    group = q_heads // kv_heads
    _, count, rows, cols = raw.shape
    copies = block_copies(spots_ref, sources, raw, sems, pl.ds(0, cols))
    for copy in copies:
        copy.start()
    for half, ref in ((half_ref[0], own_ref), (1 - half_ref[0], other_ref)):
        x = ref[...].astype(F32)
        scale = lax.rsqrt(jnp.mean(x * x, axis=-1, keepdims=True) + norm_eps)
        place = pl.ds(pl.multiple_of(half * step, step), step)
        normed[place, :] = (x * scale * gain_ref[...]).astype(BF)
    bias[...] = bias_of(length_ref, tenant_ref, 0, step, step)
    for copy in copies:
        copy.wait()
    narrow, wide = spread_ref.shape

    def turned(x):
        return (
            x * cos_ref[...]
            + pltpu.roll(x, narrow - HALF, 1) * low_ref[...]
            + pltpu.roll(x, HALF, 1) * high_ref[...]
        ).astype(BF)

    def spread(x):
        return jnp.dot(x, spread_ref[...], preferred_element_type=F32).astype(BF)

    def project(part):
        return jnp.dot(
            normed[...], raw[part].reshape(count * rows, cols), preferred_element_type=F32
        )

    key_value = project(1)
    key_heads = turned(key_value[:, :narrow])
    value_heads = key_value[:, narrow:].astype(BF)
    cache_ref[0] = key_heads
    cache_ref[1] = value_heads
    keys[...] = spread(key_heads)
    values[...] = spread(value_heads)
    query = project(0)
    for b in range(cols // narrow):
        q_wide = spread(turned(query[:, b * narrow : (b + 1) * narrow]))
        late_ref[:, b * wide : (b + 1) * wide] = q_wide[step:, :]
        for g in range(wide // LANES):
            h = b * (wide // LANES) + g
            lanes = slice(h // group * LANES, (h // group + 1) * LANES)
            mixed[:, h * LANES : (h + 1) * LANES] = attend_head(
                q_wide[:step, g * LANES : (g + 1) * LANES],
                keys[:step, lanes],
                values[:step, lanes],
                bias[...],
            )
    att_ref[...] = packed(mixed[...], pack_ref)


def late_kernel(
    q_heads, kv_heads, length_ref, tenant_ref, q_ref, keys, values, pack_ref, att_ref, mixed, bias
):
    step = q_ref.shape[0]
    seen = keys.shape[0]
    group = q_heads // kv_heads
    bias[...] = bias_of(length_ref, tenant_ref, seen - step, step, seen)
    for h in range(q_heads):
        head = slice(h * LANES, (h + 1) * LANES)
        lanes = slice(h // group * LANES, (h // group + 1) * LANES)
        mixed[:, head] = attend_head(q_ref[:, head], keys[:, lanes], values[:, lanes], bias[...])
    att_ref[...] = packed(mixed[...], pack_ref)


def block_list(refs):
    blocks = []
    for ref in refs:
        blocks += [ref] if len(ref.shape) == 2 else [ref.at[i] for i in range(ref.shape[0])]
    return blocks


def block_copies(spots_ref, sources, target, sems, cols):
    return [
        pltpu.make_async_copy(
            source.at[:, cols], target.at[spots_ref[0, s], spots_ref[1, s]], sems.at[s]
        )
        for s, source in enumerate(sources)
    ]


def attention_early(
    spots, lengths, tenants, half, own, other, gain, tables, spread, blocks, cols, q_heads, kv_heads
):
    step, width = own.shape
    tokens = 2 * step
    rows = blocks[0].shape[0]
    total = spots.shape[1]
    return pl.pallas_call(
        functools.partial(project_kernel, q_heads, kv_heads, len(blocks)),
        out_shape=(
            jax.ShapeDtypeStruct((step, q_heads * HEAD_DIM), BF),
            jax.ShapeDtypeStruct((2, tokens, kv_heads * HEAD_DIM), BF),
            jax.ShapeDtypeStruct((step, q_heads * LANES), BF),
            jax.ShapeDtypeStruct((tokens, kv_heads * LANES), BF),
            jax.ShapeDtypeStruct((tokens, kv_heads * LANES), BF),
        ),
        in_specs=[pl.BlockSpec(memory_space=pltpu.SMEM)] * 4
        + in_vmem(8)
        + [pl.BlockSpec(memory_space=pl.ANY)] * len(blocks),
        out_specs=tuple(in_vmem(5)),
        scratch_shapes=[
            pltpu.VMEM((2, total // 2, rows, cols), BF),
            pltpu.VMEM((tokens, width), BF),
            pltpu.VMEM((step, q_heads * LANES), BF),
            pltpu.VMEM((step, step), F32),
            pltpu.SemaphoreType.DMA((total,)),
        ],
        compiler_params=params(52),
        name="attention_early",
        cost_estimate=pl.CostEstimate(
            flops=4 * tokens * width * cols,
            bytes_accessed=4 * width * cols + 12 * own.size,
            transcendentals=q_heads * step * step,
        ),
    )(spots, lengths, tenants, half, own, other, gain, *tables, spread, spread.T, *blocks)


def attention_late(lengths, tenants, queries, keys, values, pack, q_heads, kv_heads):
    step, tokens = queries.shape[0], keys.shape[0]
    return pl.pallas_call(
        functools.partial(late_kernel, q_heads, kv_heads),
        out_shape=jax.ShapeDtypeStruct((step, q_heads * HEAD_DIM), BF),
        in_specs=[pl.BlockSpec(memory_space=pltpu.SMEM)] * 2 + in_vmem(4),
        out_specs=pl.BlockSpec(memory_space=pltpu.VMEM),
        scratch_shapes=[
            pltpu.VMEM((step, q_heads * LANES), BF),
            pltpu.VMEM((step, tokens), F32),
        ],
        compiler_params=params(48),
        name="attention_late",
        cost_estimate=pl.CostEstimate(
            flops=4 * q_heads * step * tokens * LANES,
            bytes_accessed=8 * keys.size,
            transcendentals=q_heads * step * tokens,
        ),
    )(lengths, tenants, queries, keys, values, pack)


def ffn_kernel(
    blocks,
    first_col,
    spots_ref,
    side_ref,
    base_ref,
    other_ref,
    w_first_ref,
    w_second_ref,
    gain_ref,
    down_ref,
    *refs,
):
    sources, refs = block_list(refs[:blocks]), refs[blocks:]
    res_ref, part_ref, buf, down_buf, normed, total, sems, down_sems = refs
    _, _, count, rows, wide = buf.shape
    width = count * rows
    steps = down_ref.shape[0] // wide

    def copies(j):
        slot = j % 2
        made = block_copies(
            spots_ref, sources, buf.at[slot], sems.at[slot], pl.ds(first_col + j * wide, wide)
        )
        made.append(
            pltpu.make_async_copy(
                down_ref.at[pl.ds(j * wide, wide), :], down_buf.at[slot], down_sems.at[slot]
            )
        )
        return made

    pending = [copies(j) for j in range(min(2, steps))]
    for made in pending:
        for copy in made:
            copy.start()
    depth = w_first_ref.shape[0]
    core = side_ref[0]
    first = pl.ds(pl.multiple_of(core * depth, LANES), depth)
    second = pl.ds(pl.multiple_of((1 - core) * depth, LANES), depth)
    x = (
        base_ref[...]
        + jnp.dot(other_ref[:, first], w_first_ref[...], preferred_element_type=F32)
        + jnp.dot(other_ref[:, second], w_second_ref[...], preferred_element_type=F32)
    )
    res_ref[...] = x
    scale = lax.rsqrt(jnp.mean(x * x, axis=-1, keepdims=True) + norm_eps)
    normed[...] = (x * scale * gain_ref[...]).astype(BF)
    for j in range(steps):
        slot = j % 2
        for copy in pending[j]:
            copy.wait()
        gate = jnp.dot(normed[...], buf[slot, 0].reshape(width, wide), preferred_element_type=F32)
        up = jnp.dot(normed[...], buf[slot, 1].reshape(width, wide), preferred_element_type=F32)
        hidden = (gate / (1.0 + jnp.exp(-gate)) * up).astype(BF)
        term = jnp.dot(hidden, down_buf[slot], preferred_element_type=F32)
        if j == 0:
            total[...] = term
        elif j + 1 < steps:
            total[...] += term
        else:
            part_ref[...] = (total[...] + term).astype(BF)
        if j + 2 < steps:
            pending.append(copies(j + 2))
            for copy in pending[-1]:
                copy.start()


def ffn_part(spots, side, base, other, w_first, w_second, gain, down, blocks, first_col):
    tokens, width = base.shape
    rows = blocks[0].shape[0]
    total = spots.shape[1]
    ff_half = down.shape[0]
    wide = min(512, ff_half)
    return pl.pallas_call(
        functools.partial(ffn_kernel, len(blocks), first_col),
        out_shape=(
            jax.ShapeDtypeStruct((tokens, width), F32),
            jax.ShapeDtypeStruct((tokens, width), BF),
        ),
        in_specs=[pl.BlockSpec(memory_space=pltpu.SMEM)] * 2
        + in_vmem(5)
        + [pl.BlockSpec(memory_space=pl.ANY)] * (1 + len(blocks)),
        out_specs=tuple(in_vmem(2)),
        scratch_shapes=[
            pltpu.VMEM((2, 2, total // 2, rows, wide), BF),
            pltpu.VMEM((2, wide, width), BF),
            pltpu.VMEM((tokens, width), BF),
            pltpu.VMEM((tokens, width), F32),
            pltpu.SemaphoreType.DMA((2, total)),
            pltpu.SemaphoreType.DMA((2,)),
        ],
        compiler_params=params(48),
        name="ffn_part",
        cost_estimate=pl.CostEstimate(
            flops=2 * tokens * width * (3 * ff_half + 2 * w_first.shape[0]),
            bytes_accessed=6 * width * ff_half + 4 * w_first.size,
            transcendentals=tokens * ff_half,
        ),
    )(spots, side, base, other, w_first, w_second, gain, down, *blocks)


def per_device(
    token_ids,
    prompt_lengths,
    tenant_ids,
    embed_table,
    attention_gain,
    qkv_weight,
    out_weight,
    ffn_gain,
    gate_up_weight,
    down_weight,
):
    tp_count = lax.axis_size("tp")
    tp_index = lax.axis_index("tp")
    group_count = lax.axis_size("req")
    req_index = lax.axis_index("req")
    tokens = token_ids.shape[0]
    looked = tokens // tp_count
    own_rows, width = embed_table.shape
    capacity = max(2, 2 * looked // group_count)
    q_half = out_weight.shape[0]
    ff_half = down_weight.shape[0]
    q_full = q_half * tp_count
    kv_half = (qkv_weight.shape[1] - q_full) // (2 * tp_count)
    kv_full = kv_half * tp_count
    ff_full = ff_half * tp_count
    chips = group_count // 2
    core = req_index % 2
    chip = req_index // 2
    core_swap = [(i, i ^ 1) for i in range(group_count)]
    order, ring_pairs = chip_ring(chips)

    my_ids = lax.dynamic_slice_in_dim(token_ids, tp_index * looked, looked)
    owner_of = my_ids // own_rows
    row_in_range = my_ids - owner_of * own_rows
    earlier = jnp.arange(looked)[None, :] < jnp.arange(looked)[:, None]
    same = (owner_of[:, None] == owner_of[None, :]) & earlier
    place = owner_of * capacity + jnp.sum(same.astype(jnp.int32), axis=1)
    slots = jnp.arange(group_count * capacity, dtype=jnp.int32)
    chosen = place[None, :] == slots[:, None]
    requests = jnp.sum(jnp.where(chosen, row_in_range[None, :] + 1, 0), axis=1) - 1
    asked = lax.all_to_all(
        requests.reshape(group_count, capacity), "req", split_axis=0, concat_axis=0, tiled=True
    ).reshape(-1)

    pick_rows = (asked[:, None] == jnp.arange(own_rows, dtype=jnp.int32)[None, :]).astype(BF)
    found_rows = jnp.dot(pick_rows, embed_table, preferred_element_type=F32).astype(BF)
    returned = lax.all_to_all(
        found_rows.reshape(group_count, capacity, width),
        "req",
        split_axis=0,
        concat_axis=0,
        tiled=True,
    ).reshape(group_count * capacity, width)
    lengths = prompt_lengths[0]
    kv_local = kv_half // HEAD_DIM
    lane = jnp.arange(kv_half, dtype=jnp.int32) % HEAD_DIM
    frequency = rope_base ** (-2.0 * (lane % HALF).astype(F32) / HEAD_DIM)
    offset = token_offsets(after(lengths, found_rows), tokens)
    angles = offset.astype(F32)[:, None] * frequency[None, :]
    sine = jnp.sin(angles)
    low = lane < HALF
    tables = (jnp.cos(angles), jnp.where(low, -sine, 0.0), jnp.where(low, 0.0, sine))

    q_parts = ((0, q_half),)
    kv_parts = ((q_full, kv_half), (q_full + kv_full, kv_half))

    def columns(half, part):
        pieces = [
            lax.dynamic_slice_in_dim(qkv_weight, base + half * size, size, axis=1)
            for base, size in (q_parts, kv_parts)[part]
        ]
        pieces.append(
            lax.dynamic_slice_in_dim(
                gate_up_weight, part * ff_full + half * ff_half, ff_half, axis=1
            )
        )
        return after(jnp.concatenate([piece.astype(BF) for piece in pieces], axis=1), *tables)

    def chip_block(parts):
        kept = jnp.where(core == 0, parts[0], parts[1])
        moved = lax.ppermute(jnp.where(core == 0, parts[1], parts[0]), "req", core_swap)
        return jnp.concatenate(
            [jnp.where(core == 0, kept, moved), jnp.where(core == 0, moved, kept)], axis=0
        )

    own_ring = [chip_block([columns(tp_index, part) for part in range(2)])]
    away = jnp.stack([columns(1 - tp_index, part) for part in range(2)])
    came = lax.ppermute(away, "tp", PAIR)
    other_ring = [chip_block([came[part] for part in range(2)])]

    steps = jnp.arange(chips, dtype=jnp.int32)
    here = jnp.where(chip % 2 == 0, chip // 2, chips - 1 - chip // 2)

    def source_chip(position):
        position = position % chips
        return jnp.where(position < (chips + 1) // 2, 2 * position, 2 * (chips - 1 - position) + 1)

    up_chip, down_chip = source_chip(here - steps), source_chip(here + steps)
    mine = jnp.where(core == 0, up_chip, down_chip)
    theirs = jnp.where(core == 0, down_chip, up_chip)
    own_row, other_row = tp_index * chips, (1 - tp_index) * chips
    spots = jnp.stack(
        [
            jnp.repeat(jnp.stack([core, 1 - core]), 2 * chips),
            jnp.concatenate(
                [own_row + mine, other_row + mine, own_row + theirs, other_row + theirs]
            ),
        ]
    ).astype(jnp.int32)

    pick_mine = (place[:, None] == slots[None, :]).astype(BF)
    embedded_own = jnp.dot(pick_mine, returned, preferred_element_type=F32).astype(BF)
    embedded_other = lax.ppermute(embedded_own, "tp", PAIR)

    out_rows = q_half // 2
    out_first = lax.ppermute(
        after(lax.dynamic_slice_in_dim(out_weight, core * out_rows, out_rows), came), "tp", PAIR
    )
    def swapped(blocks):
        sent = blocks[0] if len(blocks) == 1 else jnp.stack(blocks)
        return lax.ppermute(sent, "req", core_swap)

    cut = (chips + 2) // 2
    for i in range(chips - 1):
        ready = {2: (embedded_own,), chips - 3: (embedded_other,)}.get(i, ())
        own_ring = ring_more(own_ring, 1, ring_pairs, other_ring[max(i - 1, 0)], *ready)
        other_ring = ring_more(other_ring, 1, ring_pairs, own_ring[i])
    out_second = lax.ppermute(after(out_first, own_ring[chips - 2]), "req", core_swap)
    blocks = [
        *own_ring,
        *other_ring,
        swapped(own_ring[:cut]),
        swapped(own_ring[cut:-1]),
        swapped(own_ring[-1:]),
        swapped(other_ring[:cut]),
        swapped(other_ring[cut:-1]),
        swapped(other_ring[-1:]),
    ]

    spread = spread_columns(kv_local)
    pack = spread.T
    q_local = q_half // HEAD_DIM
    early, kv_cache, queries, keys, values = attention_early(
        spots,
        lengths,
        tenant_ids[0],
        tp_index[None],
        embedded_own,
        embedded_other,
        attention_gain[None, :],
        tables,
        spread,
        blocks,
        q_half,
        q_local,
        kv_local,
    )
    early_other = lax.ppermute(early, "tp", PAIR)
    queries = after(queries, early_other)
    late = attention_late(lengths, tenant_ids[0], queries, keys, values, pack, q_local, kv_local)
    finals = []
    late_other = lax.ppermute(late, "tp", PAIR)
    sides = ((early, early_other), (late, late_other))
    for half, (attended, came_over) in enumerate(sides):
        start = jnp.where(tp_index == half, embedded_own, embedded_other).astype(F32)
        residual, part = ffn_part(
            spots,
            core[None],
            start + jnp.dot(attended, out_weight, preferred_element_type=F32),
            came_over,
            out_first,
            out_second,
            ffn_gain[None, :],
            down_weight,
            blocks,
            q_half,
        )
        total = part.astype(F32) + lax.ppermute(part, "tp", PAIR).astype(F32)
        finals.append((residual + total).astype(BF))
    return (jnp.concatenate(finals, axis=0), kv_cache)


def solution(mesh):
    return jax.shard_map(
        per_device,
        mesh=mesh,
        in_specs=(
            P("req"),
            P("req", None),
            P("req", None),
            P("req", None),
            P(),
            P(("tp", "req"), None),
            P("tp", None),
            P(),
            P(("tp", "req"), None),
            P("tp", None),
        ),
        out_specs=(P("req", None), P(None, "req", "tp")),
        check_vma=False,
    )
```
